128 devices in a mesh: dp: 8 (over z_lo, y), sp: 16 (over x, z_hi, core).
Axes of the slice: x: 4, y: 4, z: 4 (z_hi: 2, z_lo: 2; z = z_hi * 2 + z_lo), core: 2. Of those that a mesh axis runs over, the one named last changes fastest.
Arguments:
- feats: bfloat16 [8, 32, 256, 128], P('dp', None, 'sp'), may hold values from -62 to 62
- conv_w: bfloat16 [1152, 256], replicated, may hold values from -0.1875 to 0.1875
- group_norm_gain: float32 [256], replicated, may hold values from 0.5 to 1.5
- group_norm_bias: float32 [256], replicated, may hold values from -3 to 3
- emb_w: bfloat16 [256, 3072], replicated, may hold values from -0.375 to 0.375
- time_w: bfloat16 [256, 9216], replicated, may hold values from -0.375 to 0.375
- up_w: bfloat16 [3072, 6144], P(None, 'sp'), may hold values from -0.109375 to 0.109375
- down_w: bfloat16 [6144, 3072], P('sp'), may hold values from -0.078125 to 0.078125
- steps: int32 [8], P('dp'), may hold values from 0 to 999
- cotangent: bfloat16 [8, 2048, 3072], P('dp', 'sp'), may hold values from -28 to 28
Outputs:
- grad_conv: float32 [1152, 256], replicated
- grad_up: float32 [3072, 6144], P('dp', 'sp')
- grad_down: float32 [6144, 3072], P('sp', 'dp')
The draws below stay inside these ranges and needn't reach their ends.
All inputs are finite; a program needn't handle non-finite values.
Results may differ from the reference program's by a relative error of at most 0.012.
Values may be sent and summed in bfloat16 or wider, within the bound.
A program may use at most 192 MiB of HBM per device.

```python
import math
import jax
import jax.numpy as jnp
from jax import lax

C0 = 128
C1 = 256
NORM_GROUPS = 32
DM = 3072
FF = 6144
TFREQ = 256
OH = 16
IMAGES = 8
HIN = 32
WIN = 256
OW = 128
TOKENS = 2048
KC = 1152
N_SP = 16


def draw_feats(key, part):
    base_key, row_key, col_key = jax.random.split(jax.random.fold_in(key, 101), 3)
    shape = (IMAGES, HIN, WIN, C0)
    base = jnp.clip(jax.random.normal(base_key, shape, jnp.float32), -6.0, 6.0)
    row_scale = jnp.exp(jax.random.uniform(row_key, (IMAGES, HIN, 1, 1), jnp.float32, 0.0, math.log(10.0)))
    ramp = jnp.exp(math.log(3.0) * jnp.arange(WIN, dtype=jnp.float32) / (WIN - 1))
    col_scale = ramp[None, None, :, None] * jnp.exp(jax.random.uniform(col_key, (IMAGES, 1, WIN, 1), jnp.float32, 0.0, math.log(3.4)))
    return (0.1 * base * row_scale * col_scale).astype(jnp.bfloat16)


def draw_cotangent(key, part):
    base_key, shared_key, token_key = jax.random.split(jax.random.fold_in(key, 202), 3)
    shape = (IMAGES, TOKENS, DM)
    base = jnp.clip(jax.random.normal(base_key, shape, jnp.float32), -6.0, 6.0)
    shared = 0.7 * jnp.clip(jax.random.normal(shared_key, (IMAGES, 1, DM), jnp.float32), -3.0, 3.0)
    ramp = jnp.exp(math.log(3.0) * jnp.arange(TOKENS, dtype=jnp.float32) / (TOKENS - 1))
    token_scale = ramp[None, :, None] * jnp.exp(jax.random.uniform(token_key, (IMAGES, TOKENS, 1), jnp.float32, 0.0, math.log(3.4))) / 3.0
    return ((base + shared) * token_scale).astype(jnp.bfloat16)


def set_ends(array, stream_key, smallest, largest):
    longest = array.shape.index(max(array.shape))
    spots = []
    for shift in (0, 1):
        where = [jax.random.randint(jax.random.fold_in(stream_key, axis), (), 0, length) for axis, length in enumerate(array.shape)]
        where[longest] = (where[longest] + shift) % array.shape[longest]
        spots.append(tuple(where))
    return array.at[spots[0]].set(smallest).at[spots[1]].set(largest)


def shard_levels(own_key, shape, cuts, least, top_value):
    level, own = 1.0, jax.random.fold_in(own_key, 6)
    for dim, blocks in cuts:
        heights = jnp.exp(jax.random.uniform(jax.random.fold_in(own, dim), (blocks,), jnp.float32, least / len(cuts), top_value / len(cuts)))
        level = level * jnp.repeat(heights, shape[dim] // blocks).reshape([-1 if axis == dim else 1 for axis in range(len(shape))])
    return level


def bell_draw(own_key, dims, scale, bound, shards=(), kind=jnp.bfloat16):
    factor_of = shard_levels(own_key, dims, shards, -0.22, 0.18) if shards else 1.0
    drawn = jax.random.normal(own_key, dims, jnp.float32) * scale * factor_of
    return jnp.minimum(jnp.maximum(drawn, -bound), bound).astype(kind)


def setup_inputs(seed: int = 0) -> dict:
    splits = jax.random.split(jax.random.key(seed), 11)
    feats = draw_feats(jax.random.fold_in(splits[10], 71), 0)
    conv_w = bell_draw(splits[1], (KC, C1), KC ** -0.5, 0.1875)
    group_norm_gain = jnp.clip(1.0 + 0.1 * jax.random.normal(splits[2], (C1,), jnp.float32), 0.5, 1.5)
    group_norm_bias = bell_draw(splits[3], (C1,), 0.5, 3.0, (), jnp.float32)
    emb_w = bell_draw(splits[4], (C1, DM), C1 ** -0.5, 0.375)
    time_w = bell_draw(splits[5], (TFREQ, 3 * DM), TFREQ ** -0.5, 0.375)
    up_w = bell_draw(splits[6], (DM, FF), DM ** -0.5, 0.109375, ((1, 16),))
    down_w = bell_draw(splits[7], (FF, DM), FF ** -0.5, 0.078125, ((0, 16),))
    steps = set_ends(jax.random.randint(splits[8], (IMAGES,), 0, 1000), jax.random.fold_in(splits[8], 1), 0, 999).astype(jnp.int32)
    cotangent = draw_cotangent(jax.random.fold_in(splits[10], 71), 0)
    return dict(feats=feats, conv_w=conv_w, group_norm_gain=group_norm_gain, group_norm_bias=group_norm_bias, emb_w=emb_w, time_w=time_w, up_w=up_w, down_w=down_w, steps=steps, cotangent=cotangent)


def gelu_pair(u):
    coef = math.sqrt(2.0 / math.pi)
    inner = coef * (u + 0.044715 * u * u * u)
    tangent = jnp.tanh(inner)
    value = 0.5 * u * (1.0 + tangent)
    slope = 0.5 * (1.0 + tangent) + 0.5 * u * (1.0 - tangent * tangent) * coef * (1.0 + 3.0 * 0.044715 * u * u)
    return (value, slope)

def silu_pair(value):
    sigma = jax.nn.sigmoid(value)
    return (value * sigma, sigma * (1.0 + value * (1.0 - sigma)))

def modulation(step_value, time_w):
    half = time_w.shape[0] // 2
    freqs = jnp.exp(-math.log(10000.0) * jnp.arange(half, dtype=jnp.float32) / half)
    angle = step_value.astype(jnp.float32) * freqs
    embed = jnp.concatenate([jnp.cos(angle), jnp.sin(angle)])
    mixed = jnp.dot(jax.nn.silu(embed).astype(jnp.bfloat16)[None, :], time_w, preferred_element_type=jnp.float32)[0]
    width = time_w.shape[1] // 3
    return (mixed[:width], mixed[width:2 * width], mixed[2 * width:])

def make_patches(padded, rows, cols):
    pieces = []
    for row_tap in range(3):
        for col_tap in range(3):
            pieces.append(padded[row_tap:row_tap + 2 * rows:2, col_tap:col_tap + 2 * cols:2, :])
    stacked = jnp.concatenate(pieces, axis=-1)
    return stacked.reshape(rows * cols, stacked.shape[-1])

def group_totals(first, second, groups):
    tokens, width = first.shape
    first_g = first.reshape(tokens, groups, width // groups)
    second_g = second.reshape(tokens, groups, width // groups)
    return (lax.optimization_barrier(jnp.sum(first_g, axis=(0, 2))), lax.optimization_barrier(jnp.sum(second_g, axis=(0, 2))))

def broadcast_groups(values, width):
    return jnp.repeat(values, width // values.shape[0])

def bf16_round(values):
    return lax.optimization_barrier(values.astype(jnp.bfloat16)).astype(jnp.float32)

def contract(left, right, left_dim, right_dim):
    return lax.dot_general(left, right, (((left_dim,), (right_dim,)), ((), ())), preferred_element_type=jnp.float32)

def reference(feats, conv_w, group_norm_gain, group_norm_bias, emb_w, time_w, up_w, down_w, steps, cotangent):
    channel_count = conv_w.shape[1]
    slice_width = FF // N_SP
    grad_conv = jnp.zeros(conv_w.shape, jnp.float32)
    grad_up = jnp.zeros(up_w.shape, jnp.float32)
    grad_down = jnp.zeros(down_w.shape, jnp.float32)
    for image_index in range(IMAGES):
        image = feats[image_index]
        padded = jnp.pad(image, ((1, 0), (1, 0), (0, 0)))
        patches = make_patches(padded, OH, OW)
        normed_value = jnp.dot(patches, conv_w, preferred_element_type=jnp.float32)
        first, second = group_totals(normed_value, normed_value * normed_value, NORM_GROUPS)
        group_count = normed_value.shape[0] * (channel_count // NORM_GROUPS)
        group_mean = first / group_count
        rstd = lax.rsqrt(second / group_count - group_mean * group_mean + 1e-05)
        channel_rstd = broadcast_groups(rstd, channel_count)
        centered_input = (normed_value - broadcast_groups(group_mean, channel_count)) * channel_rstd
        preactivation = centered_input * group_norm_gain + group_norm_bias
        act_val, silu_slope = silu_pair(preactivation)
        act_b = act_val.astype(jnp.bfloat16)
        shift, scale, gate = modulation(steps[image_index], time_w)
        hidden_in = jnp.dot(act_b, emb_w, preferred_element_type=jnp.float32)
        centered = hidden_in - lax.optimization_barrier(jnp.mean(hidden_in, axis=-1, keepdims=True))
        token_rstd = lax.rsqrt(lax.optimization_barrier(jnp.mean(centered * centered, axis=-1, keepdims=True)) + 1e-06)
        hhat = centered * token_rstd
        normed = (hhat * (1.0 + scale) + shift).astype(jnp.bfloat16)
        upper = jnp.dot(normed, up_w, preferred_element_type=jnp.float32)
        gelu_val, gelu_slope = gelu_pair(upper)
        hid = gelu_val.astype(jnp.bfloat16)
        cot = cotangent[image_index].astype(jnp.float32)
        scaled_cot = (cot * gate).astype(jnp.bfloat16)
        dhid = contract(scaled_cot, down_w, 1, 1)
        dupper = (dhid * gelu_slope).astype(jnp.bfloat16)
        grad_down = grad_down + bf16_round(contract(hid, scaled_cot, 0, 0))
        grad_up = grad_up + bf16_round(contract(normed, dupper, 0, 0))

        def block_term(total, block):
            start = block * slice_width
            du_block = lax.dynamic_slice_in_dim(dupper, start, slice_width, 1)
            w_block = lax.dynamic_slice_in_dim(up_w, start, slice_width, 1)
            return (total + bf16_round(contract(du_block, w_block, 1, 1)), None)
        dnormed, _ = lax.scan(block_term, jnp.zeros((normed.shape[0], DM), jnp.float32), jnp.arange(N_SP, dtype=jnp.int32))
        dhh = dnormed * (1.0 + scale)
        dhh_mean = lax.optimization_barrier(jnp.mean(dhh, axis=-1, keepdims=True))
        dhh_cross = lax.optimization_barrier(jnp.mean(dhh * hhat, axis=-1, keepdims=True))
        dh_val = (cot + token_rstd * (dhh - dhh_mean - hhat * dhh_cross)).astype(jnp.bfloat16)
        dact = contract(dh_val, emb_w, 1, 1)
        input_gradient = dact * silu_slope * group_norm_gain
        backward_first, backward_second = group_totals(input_gradient, input_gradient * centered_input, NORM_GROUPS)
        normed_gradient = (channel_rstd * (input_gradient - broadcast_groups(backward_first / group_count, channel_count) - centered_input * broadcast_groups(backward_second / group_count, channel_count))).astype(jnp.bfloat16)
        grad_conv = grad_conv + contract(patches, normed_gradient, 0, 0)
    return (grad_conv, grad_up, grad_down)
```

```python
import math

import jax
import jax.numpy as jnp
from jax import lax
from jax.sharding import Mesh
from jax.sharding import PartitionSpec as P

NORM_GROUPS = 32
SP = ("sp_0", "sp_1", "sp_2")
DP_SP = ("dp", "sp_0", "sp_1", "sp_2")


def from_behind(array, axis, by):
    length = lax.axis_size(axis)
    pairs = [(i, i + by) for i in range(length) if 0 <= i + by < length]
    return lax.ppermute(array, axis, pairs)


def copy_for_each(array, axis):
    length = lax.axis_size(axis)
    return lax.all_to_all(
        jnp.broadcast_to(array[None], (length, *array.shape)), axis, 0, 0, tiled=True
    )


def over_copies(array, axis):
    return copy_for_each(array, axis).sum(axis=0)


def in_one(arrays, axis):
    ends = [0]
    for a in arrays:
        ends.append(ends[-1] + a.size)
    subtotal = over_copies(jnp.concatenate([a.ravel() for a in arrays]), axis)
    return tuple((subtotal[b:e].reshape(a.shape) for a, b, e in zip(arrays, ends, ends[1:])))


def in_blocks(array, dim, length):
    before, after = (array.shape[:dim], array.shape[dim + 1 :])
    return jnp.moveaxis(array.reshape(*before, length, -1, *after), dim, 0)


def sum_by_chip(array, chips, core, dim):
    sizes = (lax.axis_size(chips), lax.axis_size(core))
    parts = in_blocks(array, dim, sizes[0] * sizes[1])
    inside = parts.shape[1:]
    parts = parts.reshape(*sizes, *inside).swapaxes(0, 1).reshape(-1, *inside)
    parts = lax.psum_scatter(parts, core, scatter_dimension=0, tiled=True)
    return lax.psum_scatter(parts, chips, scatter_dimension=0, tiled=True)[0]


def sum_packed(arrays, axis, dims):
    length = lax.axis_size(axis)
    parts = [in_blocks(a, dim, length) for a, dim in zip(arrays, dims)]
    lines = jnp.concatenate([b.reshape(length, -1) for b in parts], axis=1)
    rows = max(16, -(-lines.shape[1] // 1024) * 8)
    lines = jnp.pad(lines, ((0, 0), (0, rows * 128 - lines.shape[1]))).reshape(-1, 128)
    ravelled, at, finished = (lax.psum_scatter(lines, axis, tiled=True).reshape(-1), 0, [])
    for b in parts:
        part = b[0]
        finished.append(ravelled[at : at + part.size].reshape(part.shape))
        at += part.size
    return tuple(finished)


def gelu_pair(u):
    coef = math.sqrt(2.0 / math.pi)
    inner = coef * (u + 0.044715 * u * u * u)
    tangent = jnp.tanh(inner)
    value = 0.5 * u * (1.0 + tangent)
    slope = 0.5 * (1.0 + tangent) + 0.5 * u * (1.0 - tangent * tangent) * coef * (
        1.0 + 3.0 * 0.044715 * u * u
    )
    return (value, slope)


def silu_pair(value):
    sigma = jax.nn.sigmoid(value)
    return (value * sigma, sigma * (1.0 + value * (1.0 - sigma)))


def modulation(step_value, time_w):
    half = time_w.shape[0] // 2
    freqs = jnp.exp(-math.log(10000.0) * jnp.arange(half, dtype=jnp.float32) / half)
    angle = step_value.astype(jnp.float32) * freqs
    embed = jnp.concatenate([jnp.cos(angle), jnp.sin(angle)])
    mixed = jnp.dot(
        jax.nn.silu(embed).astype(jnp.bfloat16)[None, :], time_w, preferred_element_type=jnp.float32
    )[0]
    width = time_w.shape[1] // 3
    return (mixed[:width], mixed[width : 2 * width], mixed[2 * width :])


def make_patches(padded, rows, cols):
    pieces = []
    for row_tap in range(3):
        for col_tap in range(3):
            pieces.append(
                padded[row_tap : row_tap + 2 * rows : 2, col_tap : col_tap + 2 * cols : 2, :]
            )
    stacked = jnp.concatenate(pieces, axis=-1)
    return stacked.reshape(rows * cols, stacked.shape[-1])


def group_totals(first, second, groups):
    tokens, width = first.shape
    first_g = first.reshape(tokens, groups, width // groups)
    second_g = second.reshape(tokens, groups, width // groups)
    return (jnp.sum(first_g, axis=(0, 2)), jnp.sum(second_g, axis=(0, 2)))


def broadcast_groups(values, width):
    return jnp.repeat(values, width // values.shape[0])


def contract(left, right, left_dim, right_dim):
    return lax.dot_general(
        left, right, (((left_dim,), (right_dim,)), ((), ())), preferred_element_type=jnp.float32
    )


def on_device(
    feats, conv_w, group_norm_gain, group_norm_bias, emb_w, time_w, up_w, down_w, steps, cotangent
):
    devices_sp = lax.axis_size(SP)
    image = feats[0]
    rows_in, cols_in, _ = image.shape
    rows = rows_in // 2
    cols = cols_in // 2
    seq_rows = rows // devices_sp
    channel_count = conv_w.shape[1]
    rim = from_behind(image[:, cols_in - 1, :], SP, 1)
    widened = jnp.concatenate([rim[:, None, :], image], axis=1)
    padded = jnp.pad(widened, ((1, 0), (0, 0), (0, 0)))
    patches = make_patches(padded, rows, cols)
    normed_value = jnp.dot(patches, conv_w, preferred_element_type=jnp.float32)
    first, second = group_totals(normed_value, normed_value * normed_value, NORM_GROUPS)
    first, second = in_one((first, second), SP)
    group_count = normed_value.shape[0] * devices_sp * (channel_count // NORM_GROUPS)
    group_mean = first / group_count
    rstd = lax.rsqrt(second / group_count - group_mean * group_mean + 1e-05)
    channel_rstd = broadcast_groups(rstd, channel_count)
    centered_input = (normed_value - broadcast_groups(group_mean, channel_count)) * channel_rstd
    preactivation = centered_input * group_norm_gain + group_norm_bias
    act_val, silu_slope = silu_pair(preactivation)
    act_b = act_val.astype(jnp.bfloat16)
    shift, scale, gate = modulation(steps[0], time_w)
    cot_seq = cotangent[0]
    width = emb_w.shape[1]
    all_cot = lax.all_gather(cot_seq, SP, axis=0, tiled=True)
    all_act = lax.all_gather(act_b.reshape(rows, cols, channel_count), SP, axis=1, tiled=True)
    all_act = all_act.reshape(rows * cols * devices_sp, channel_count)
    emb_f = emb_w.astype(jnp.float32)
    emb_mean = jnp.mean(emb_f, axis=1, keepdims=True)
    gram = contract(emb_w, emb_w, 1, 1) - width * emb_mean * emb_mean.T
    gram_hi = gram.astype(jnp.bfloat16)
    gram_lo = (gram - gram_hi.astype(jnp.float32)).astype(jnp.bfloat16)
    emb_c = emb_f - emb_mean
    mixer = jnp.dot(
        (emb_c * (1.0 + scale)).astype(jnp.bfloat16), up_w, preferred_element_type=jnp.float32
    ).astype(jnp.bfloat16)
    shift_hi = shift.astype(jnp.bfloat16)
    shift_lo = (shift - shift_hi.astype(jnp.float32)).astype(jnp.bfloat16)
    offset = jnp.dot(
        jnp.stack([shift_hi, shift_lo]), up_w, preferred_element_type=jnp.float32
    ).sum(axis=0)
    act_gram = jnp.dot(all_act, gram_hi, preferred_element_type=jnp.float32) + jnp.dot(
        all_act, gram_lo, preferred_element_type=jnp.float32
    )
    token_var = jnp.sum(all_act.astype(jnp.float32) * act_gram, axis=-1, keepdims=True) / width
    token_rstd = lax.rsqrt(token_var + 1e-06)
    moved = token_rstd * jnp.dot(all_act, mixer, preferred_element_type=jnp.float32)
    gelu_val, gelu_slope = gelu_pair(moved + offset)
    hid = gelu_val.astype(jnp.bfloat16)
    dhid = contract(all_cot, (down_w.astype(jnp.float32) * gate).astype(jnp.bfloat16), 1, 1)
    dupper = dhid * gelu_slope
    dupper_sum = jnp.sum(dupper, axis=0)
    dupper_r = (dupper * token_rstd).astype(jnp.bfloat16)
    cross = jnp.sum(dupper_r.astype(jnp.float32) * moved, axis=-1, keepdims=True)
    part = contract(dupper_r, mixer, 1, 1) - cross * token_rstd * act_gram / width
    dact = sum_by_chip(part.astype(jnp.bfloat16), ("sp_0", "sp_1"), "sp_2", 0).astype(jnp.float32)
    dact = dact + contract(cot_seq, emb_w, 1, 1)
    pair = contract(all_act, dupper_r, 0, 0).astype(jnp.bfloat16)
    grad_down_local = contract(hid, all_cot, 0, 0) * gate
    (grad_down,) = sum_packed((grad_down_local.astype(jnp.bfloat16),), "dp", (1,))
    grad_down = grad_down.astype(jnp.float32)
    all_pair = lax.all_gather(pair, "dp", axis=0, tiled=True)
    side = lax.all_gather(jnp.concatenate([1.0 + scale, shift, dupper_sum]), "dp", axis=0)
    here = lax.axis_index("dp")
    block = width // lax.axis_size("dp")
    emb_here = lax.dynamic_slice_in_dim(emb_c, here * block, block, 1)
    scale_here = lax.dynamic_slice_in_dim(side[:, :width], here * block, block, 1)
    shift_here = lax.dynamic_slice_in_dim(side[:, width : 2 * width], here * block, block, 1)
    left = (emb_here[None] * scale_here[:, None, :]).astype(jnp.bfloat16)
    grad_up = contract(left.reshape(-1, block), all_pair, 0, 0) + lax.dot_general(
        shift_here, side[:, 2 * width :], (((0,), (0,)), ((), ())), precision=lax.Precision.HIGHEST
    )
    back_tiles = lax.all_to_all(
        dact.reshape(seq_rows, cols * devices_sp, channel_count).astype(jnp.bfloat16),
        SP,
        split_axis=1,
        concat_axis=0,
        tiled=True,
    ).astype(jnp.float32)
    dact_tile = back_tiles.reshape(rows * cols, channel_count)
    input_gradient = dact_tile * silu_slope * group_norm_gain
    backward_first, backward_second = group_totals(
        input_gradient, input_gradient * centered_input, NORM_GROUPS
    )
    backward_first, backward_second = in_one((backward_first, backward_second), SP)
    normed_gradient = (
        channel_rstd
        * (
            input_gradient
            - broadcast_groups(backward_first / group_count, channel_count)
            - centered_input * broadcast_groups(backward_second / group_count, channel_count)
        )
    ).astype(jnp.bfloat16)
    conv_local = contract(patches, normed_gradient, 0, 0)
    grad_conv = lax.psum(conv_local, DP_SP)
    return (grad_conv, grad_up, grad_down)


def solution(mesh):
    finer = Mesh(mesh.devices.reshape(mesh.shape["dp"], 4, 2, 2), ("dp", "sp_0", "sp_1", "sp_2"))
    in_specs = (
        P("dp", None, SP, None),
        P(),
        P(),
        P(),
        P(),
        P(),
        P(None, SP),
        P(SP, None),
        P("dp"),
        P("dp", SP, None),
    )
    out_specs = (P(), P("dp", SP), P(SP, "dp"))
    return jax.shard_map(
        on_device, mesh=finer, in_specs=in_specs, out_specs=out_specs, check_vma=False
    )
```

```python
import functools
import math

import jax
import jax.numpy as jnp
from jax import lax
from jax.experimental import pallas as pl
from jax.experimental.pallas import tpu as pltpu
from jax.sharding import PartitionSpec as P

NORM_GROUPS = 32
F32 = jnp.float32
BF16 = jnp.bfloat16
MESH = pl.DeviceIdType.MESH


def gelu_pair(u):
    coef = math.sqrt(2.0 / math.pi)
    inner = coef * (u + 0.044715 * u * u * u)
    tangent = jnp.tanh(inner)
    value = 0.5 * u * (1.0 + tangent)
    slope = 0.5 * (1.0 + tangent) + 0.5 * u * (1.0 - tangent * tangent) * coef * (
        1.0 + 3.0 * 0.044715 * u * u
    )
    return (value, slope)


def nn(left, right):
    return lax.dot_general(left, right, (((1,), (0,)), ((), ())), preferred_element_type=F32)


def nt(left, right):
    return lax.dot_general(left, right, (((1,), (1,)), ((), ())), preferred_element_type=F32)


def exact(left, right, dims):
    return lax.dot_general(
        left,
        right,
        (dims, ((), ())),
        precision=lax.Precision.HIGHEST,
        preferred_element_type=F32,
    )


def split(value):
    high = value.astype(BF16)
    return high, (value - high.astype(F32)).astype(BF16)


def rows_of(first, second, like):
    which = lax.broadcasted_iota(jnp.int32, like, 0)
    return jnp.where(which == 0, first, jnp.where(which == 1, second, 0.0))


def body(
    n_sp, n_dp, es, gain_bias, patches_in, conv_in, emb_in, time_in, up_in, down_in, cot_in,
    out_conv, out_up, out_down, s,
):
    n_chip = n_sp // 2
    width = emb_in.shape[1]
    hidden = up_in.shape[1]
    block = width // n_dp
    chans = conv_in.shape[1]
    pixels = patches_in.shape[0]
    half = pixels // 2
    taps = conv_in.shape[0] // n_sp
    me = lax.axis_index("sp")
    image = lax.axis_index("dp")
    core = lax.rem(me, 2)
    chip = me // 2
    far = lax.rem(chip, 2)
    col = chip // 2
    n_col = n_chip // 2
    east_col, west_col = lax.rem(col + 1, n_col), lax.rem(col + n_col - 1, n_col)
    over_col = lax.rem(col + 2, n_col)
    sibling = chip * 2 + 1 - core
    chip_of = lambda at, level: at * 2 + level
    dev_of = lambda which: which * 2 + core
    z_chip = chip_of(col, 1 - far)
    east, west = dev_of(chip_of(east_col, far)), dev_of(chip_of(west_col, far))
    z_peer = dev_of(z_chip)

    def send(src, dst, sems, at_send, at_recv, **where):
        return pltpu.make_async_remote_copy(
            src_ref=src, dst_ref=dst, send_sem=sems.at[0, at_send], recv_sem=sems.at[1, at_recv],
            device_id=where, device_id_type=MESH,
        )

    def others(count, first, act):
        @pl.loop(1, count)
        def _(step):
            act(lax.rem(first + step, count))

    def every(count, act):
        @pl.loop(0, count)
        def _(step):
            act(step)

    barrier = pltpu.get_barrier_semaphore()
    others(n_sp, me, lambda p: pl.semaphore_signal(barrier, 1, device_id={"sp": p}, device_id_type=MESH))
    others(n_dp, image, lambda p: pl.semaphore_signal(barrier, 1, device_id={"dp": p}, device_id_type=MESH))

    loads = {}
    for index, (name, src, dst) in enumerate(
        (
            ("patches", patches_in, s.patches),
            ("conv", conv_in, s.conv),
            ("emb", emb_in, s.emb),
            ("up", up_in, s.up),
        )
    ):
        loads[name] = pltpu.make_async_copy(src, dst, s.load.at[index])

    def cot_load(p):
        columns = pl.ds(pl.multiple_of(p * block, block), block)
        return pltpu.make_async_copy(cot_in.at[:, columns], s.cot.at[p, chip], s.load.at[8 + p])

    my_rows = pl.ds(pl.multiple_of(core * hidden, hidden), hidden)
    its_rows = pl.ds(pl.multiple_of((1 - core) * hidden, hidden), hidden)

    def down_load(p):
        columns = pl.ds(pl.multiple_of(p * block, block), block)
        return pltpu.make_async_copy(
            down_in.at[:, columns], s.gated.at[p, my_rows], s.load.at[8 + n_dp + p]
        )

    def time_load(k):
        columns = pl.ds(pl.multiple_of(k * 1024, 1024), 1024)
        slot = lax.rem(k, 2)
        return pltpu.make_async_copy(time_in.at[:, columns], s.time.at[slot], s.load.at[6 + slot])

    loads["patches"].start()
    loads["conv"].start()
    every(n_dp, lambda p: cot_load(p).start())
    every(n_dp, lambda p: down_load(p).start())
    time_load(0).start()
    for name in ("emb", "up"):
        loads[name].start()

    loads["patches"].wait()
    loads["conv"].wait()
    s.z[...] = nn(s.patches[...], s.conv[...])
    z = s.z[...]
    s.stat_tx[...] = rows_of(
        jnp.sum(z, axis=0, keepdims=True), jnp.sum(z * z, axis=0, keepdims=True), (8, chans)
    )
    s.stat_rx[me] = s.stat_tx[...]

    pl.semaphore_wait(barrier, n_sp - 1 + n_dp - 1)

    def stat_copy(p):
        return send(s.stat_tx, s.stat_rx.at[me], s.stat_sem, p, me, sp=p)

    def stat_from(p):
        return send(s.stat_tx, s.stat_rx.at[p], s.stat_sem, p, p, sp=p)

    others(n_sp, me, lambda p: stat_copy(p).start())

    every(n_dp, lambda p: cot_load(p).wait())

    def turn(q):
        return lax.rem(image + 1 + q, n_dp)

    top, low = pl.ds(0, half), pl.ds(half, half)
    routes = {
        "z": (chip, None, z_peer, z_chip),
        "e": (chip, None, east, chip_of(west_col, far)),
        "w": (chip, None, west, chip_of(east_col, far)),
        "ez": (z_chip, None, east, chip_of(west_col, 1 - far)),
        "wz": (z_chip, None, west, chip_of(east_col, 1 - far)),
        "ee": (chip_of(west_col, far), top, east, chip_of(over_col, far)),
        "ww": (chip_of(east_col, far), low, west, chip_of(over_col, far)),
        "eez": (chip_of(west_col, 1 - far), top, east, chip_of(over_col, 1 - far)),
        "wwz": (chip_of(east_col, 1 - far), low, west, chip_of(over_col, 1 - far)),
    }
    order = {name: index for index, name in enumerate(routes)}

    def cot_copy(name, p, arriving=False):
        mine, part, to, theirs = routes[name]
        which = theirs if arriving else mine
        ref = s.cot.at[p, which] if part is None else s.cot.at[p, which, part, :]
        at = order[name] * n_dp + p
        return send(ref, ref, s.cot_sem, at, at, sp=to)

    def own(q):
        p = turn(q)
        for name in ("z", "e", "w"):
            cot_copy(name, p).start()

    def relay(q):
        p = turn(q)
        for name, then in (
            ("z", ("ez", "wz")),
            ("e", ("ee",)),
            ("w", ("ww",)),
            ("ez", ("eez",)),
            ("wz", ("wwz",)),
        ):
            cot_copy(name, p, True).wait_recv()
            for onward in then:
                cot_copy(onward, p).start()

    def landed(q):
        p = turn(q)
        for name in ("ee", "ww", "eez", "wwz"):
            cot_copy(name, p, True).wait_recv()

    own(0)
    own(1)

    every(n_dp, lambda p: down_load(p).wait())
    my_down, its_down = s.gated.at[:, my_rows], s.gated.at[:, its_rows]
    down_copy = send(my_down, my_down, s.pair_sem, 0, 0, sp=sibling)
    down_copy.start()

    n_time = 3 * width // 1024

    def mod_part(k):
        @pl.when(k + 1 < n_time)
        def _():
            time_load(k + 1).start()

        columns = pl.ds(pl.multiple_of(k * 1024, 1024), 1024)
        time_load(k).wait()
        s.mod[:, columns] = nn(es[...], s.time[lax.rem(k, 2)])

    every(n_time, mod_part)

    others(n_sp, me, lambda p: stat_from(p).wait_recv())
    count = pixels * n_sp * (chans // NORM_GROUPS)
    shift_by = (chans // NORM_GROUPS).bit_length() - 1

    def group_sums(ref):
        pair = lax.broadcasted_iota(jnp.int32, (chans, chans), 0) >> shift_by
        other = lax.broadcasted_iota(jnp.int32, (chans, chans), 1) >> shift_by
        same = jnp.where(pair == other, 1.0, 0.0).astype(F32)
        totals = exact(jnp.sum(ref[...], axis=0), same, ((1,), (0,))) / count
        return totals[0:1, :], totals[1:2, :]

    mean, square = group_sums(s.stat_rx)
    rstd = lax.rsqrt(square - mean * mean + 1e-05)
    s.rstd[...] = jnp.broadcast_to(rstd, s.rstd.shape)
    xhat = (s.z[...] - mean) * rstd
    s.z[...] = xhat
    pre = xhat * gain_bias[0:1, :] + gain_bias[1:2, :]
    sigma = jax.nn.sigmoid(pre)
    s.slope0[...] = sigma * (1.0 + pre * (1.0 - sigma)) * gain_bias[0:1, :]
    act = (pre * sigma).reshape(n_chip, 2, pixels // n_sp, chans)
    for k in range(2):
        s.act_tx[k] = act[:, k].reshape(half, chans).astype(BF16)
    s.act_rx[me] = s.act_tx[core]

    def act_copy(p, source):
        return send(s.act_tx.at[lax.rem(p, 2)], s.act_rx.at[source], s.act_sem, p, source, sp=p)

    others(n_sp, me, lambda p: act_copy(p, me).start())
    own(2)
    relay(0)

    loads["emb"].wait()
    loads["up"].wait()
    ones = jnp.ones((16, width), BF16)
    mean_row = nt(ones, s.emb[...])[0:1, :] / width
    s.mean_col[...] = jnp.broadcast_to(
        jnp.mean(s.emb[...].astype(F32), axis=1, keepdims=True), s.mean_col.shape
    )
    mean_col = s.mean_col[:, 0:1]
    s.gram[...] = jnp.zeros_like(s.gram)
    s.mix[...] = jnp.zeros_like(s.mix)
    s.offset[...] = jnp.zeros_like(s.offset)
    s.skip[...] = jnp.zeros_like(s.skip)

    def fold(p):
        columns = pl.ds(pl.multiple_of(p * block, block), block)
        emb = s.emb[:, columns]
        scale = s.mod[0:1, pl.ds(pl.multiple_of(width + p * block, block), block)]
        left = ((emb.astype(F32) - mean_col) * (1.0 + scale)).astype(BF16)
        up = s.up[columns, :]
        s.mix[...] += nn(left, up)
        s.gram[...] += nt(emb, emb)
        high, low_part = split(s.mod[:, columns])
        s.offset[...] += nn(high, up) + nn(low_part, up)
        s.skip[...] += nt(s.cot[p, chip], emb)

    every(n_dp, fold)
    my_cols, its_cols = my_rows, its_rows
    s.mixer[:, my_cols] = s.mix[...].astype(BF16)
    s.offsets[:, my_cols] = s.offset[...]
    mix_copy = send(s.mixer.at[:, my_cols], s.mixer.at[:, my_cols], s.pair_sem, 1, 1, sp=sibling)
    mix_copy.start()
    off_copy = send(s.offsets.at[:, my_cols], s.offsets.at[:, my_cols], s.pair_sem, 2, 2, sp=sibling)
    off_copy.start()
    own(3)
    relay(1)

    down_from = send(its_down, its_down, s.pair_sem, 0, 0, sp=sibling)
    down_copy.wait_send()
    down_from.wait_recv()

    def gate_part(p):
        gate = s.mod[0:1, pl.ds(pl.multiple_of(2 * width + p * block, block), block)]
        s.gated[p] = (s.gated[p].astype(F32) * gate).astype(BF16)

    every(n_dp, gate_part)

    others(n_sp, me, lambda p: act_copy(p, p).wait_recv())

    def place(p):
        tile = s.act_rx[p].astype(F32).reshape(n_chip, pixels // n_sp, chans)
        s.act[:, pl.ds(pl.multiple_of(p * 8, 8), 8), :] = tile

    every(n_sp, place)
    mix_from = send(s.mixer.at[:, its_cols], s.mixer.at[:, its_cols], s.pair_sem, 1, 1, sp=sibling)
    off_from = send(s.offsets.at[:, its_cols], s.offsets.at[:, its_cols], s.pair_sem, 2, 2, sp=sibling)
    mix_from.wait_recv()
    off_from.wait_recv()
    gram_hi, gram_lo = split(s.gram[...] - width * mean_col * mean_row)
    s.gram_hi[...] = gram_hi
    s.gram_lo[...] = gram_lo

    def forward(i):
        lanes = pl.ds(pl.multiple_of(i * pixels, pixels), pixels)
        wide = s.act[i]
        narrow = wide.astype(BF16)
        spread = nn(narrow, s.gram_hi[...]) + nn(narrow, s.gram_lo[...])
        var = jnp.sum(wide * spread, axis=-1, keepdims=True) / width
        token_rstd = lax.rsqrt(var + 1e-06)
        moved = nn(narrow, s.mixer[...]) * token_rstd
        value, slope = gelu_pair(moved + s.offsets[0:1, :])
        s.hid_t[:, lanes] = value.T.astype(BF16)
        s.act_t[:, lanes] = wide.T.astype(BF16)
        s.slope[i] = slope
        s.moved[i] = moved
        s.spread[i] = spread * (token_rstd / width)
        s.token_rstd[i] = jnp.broadcast_to(token_rstd, (pixels, 128))
        s.dhid[i] = jnp.zeros_like(slope)

    every(n_chip, forward)
    s.patches_t[...] = s.patches[...].astype(F32).T.astype(BF16)

    def sib_copy(p):
        return send(s.sib_tx.at[p], s.sib_rx.at[p], s.sib_sem, p, p, sp=sibling)

    def down_out(p, source, to):
        return send(s.gd_tx.at[p], s.gd_rx.at[source], s.gd_sem, p, source, dp=to)

    def block_of(q):
        p = turn(q)
        gate = s.mod[0:1, pl.ds(pl.multiple_of(2 * width + p * block, block), block)]
        cot = s.cot[p].reshape(n_chip * pixels, block)
        s.sib_tx[p] = (nn(s.hid_t[its_rows, :], cot) * gate).astype(BF16)
        sib_copy(p).start()
        s.gd_own[lax.rem(q, 2)] = nn(s.hid_t[my_rows, :], cot) * gate

        def part(h):
            rows = pl.ds(h * (n_chip // 2), n_chip // 2)
            tokens = s.cot[p, rows].reshape(n_chip // 2 * pixels, block)
            s.dhid[rows] += nt(tokens, s.gated[p]).reshape(n_chip // 2, pixels, 2 * hidden)

        every(2, part)

    def whole(q):
        p = turn(q)
        sib_copy(p).wait_recv()
        return p, s.gd_own[lax.rem(q, 2)] + s.sib_rx[p].astype(F32)

    def hand_over(q):
        p, total = whole(q)
        s.gd_tx[p] = total.astype(BF16)
        down_out(p, image, p).start()

    @pl.loop(0, n_dp)
    def _(q):
        @pl.when(q + 4 < n_dp)
        def _():
            own(q + 4)

        @pl.when(q + 2 < n_dp)
        def _():
            relay(q + 2)

        @pl.when(q > 0)
        def _():
            hand_over(q - 1)

        landed(q)
        block_of(q)

    s.du_sum[...] = jnp.zeros_like(s.du_sum)

    def backward(i):
        grad = s.dhid[i] * s.slope[i]
        s.du_sum[0:1, :] += jnp.sum(grad, axis=0, keepdims=True)
        grad = grad * s.token_rstd[i][:, 0:1]
        cross = jnp.sum(grad * s.moved[i], axis=-1, keepdims=True)
        narrow = grad.astype(BF16)
        s.du[pl.ds(pl.multiple_of(i * pixels, pixels), pixels), :] = narrow
        s.act[i] = nt(narrow, s.mixer[...]) - cross * s.spread[i]

    every(n_chip, backward)
    s.act[chip] += s.skip[...]

    def tile_of(p):
        rows = s.act[:, pl.ds(pl.multiple_of(p * 8, 8), 8), :]
        return rows.reshape(half, chans).astype(BF16)

    def part_copy(p, source):
        return send(s.part_tx.at[p], s.part_rx.at[source], s.part_sem, p, source, sp=p)

    def part_out(p):
        s.part_tx[p] = tile_of(p)
        part_copy(p, me).start()

    others(n_sp, me, part_out)
    s.part_rx[me] = tile_of(me)

    s.pairs[...] = nn(s.act_t[...], s.du[...])
    s.pair_tx[...] = s.pairs[:, its_cols].astype(BF16)
    s.sum_tx[...] = s.du_sum[:, its_cols]
    pair_copy = send(s.pair_tx, s.pair_rx, s.pair_sem, 3, 3, sp=sibling)
    pair_copy.start()
    sum_copy = send(s.sum_tx, s.sum_rx, s.pair_sem, 4, 4, sp=sibling)
    sum_copy.start()
    _, total = whole(n_dp - 1)
    out_down[...] = total

    others(n_sp, me, lambda p: part_copy(p, p).wait_recv())
    parts = []
    for k in range(2):
        total = s.part_rx[k].astype(F32)
        for j in range(1, n_chip):
            total = total + s.part_rx[2 * j + k].astype(F32)
        parts.append(total.reshape(n_chip, 1, pixels // n_sp, chans))
    dx = jnp.concatenate(parts, axis=1).reshape(pixels, chans) * s.slope0[...]
    s.slope0[...] = dx
    s.stat2_tx[...] = rows_of(
        jnp.sum(dx, axis=0, keepdims=True), jnp.sum(dx * s.z[...], axis=0, keepdims=True), (8, chans)
    )
    s.stat2_rx[me] = s.stat2_tx[...]

    def stat2_copy(p, source):
        return send(s.stat2_tx, s.stat2_rx.at[source], s.stat2_sem, p, source, sp=p)

    others(n_sp, me, lambda p: stat2_copy(p, me).start())

    pair_copy.wait_recv()
    sum_copy.wait_recv()
    s.q_tx[...] = (s.pairs[:, my_cols] + s.pair_rx[...].astype(F32)).astype(BF16)
    s.q_rx[image] = s.q_tx[...]
    du_sum = (s.du_sum[:, my_cols] + s.sum_rx[...])[0:1, :]

    def side_of(p):
        shift = s.mod[0:1, pl.ds(pl.multiple_of(p * block, block), block)]
        scale = s.mod[0:1, pl.ds(pl.multiple_of(width + p * block, block), block)]
        which = lax.broadcasted_iota(jnp.int32, (8, block), 0)
        return jnp.where(which == 2, du_sum, rows_of(1.0 + scale, shift, (8, block)))

    def q_copy(p, source):
        return send(s.q_tx, s.q_rx.at[source], s.q_sem, p, source, dp=p)

    def side_copy(p, source):
        return send(s.side_tx.at[p], s.side_rx.at[source], s.side_sem, p, source, dp=p)

    def q_out(p):
        q_copy(p, image).start()
        s.side_tx[p] = side_of(p)
        side_copy(p, image).start()

    others(n_dp, image, q_out)
    s.side_rx[image] = side_of(image)

    others(n_sp, me, lambda p: stat2_copy(p, p).wait_recv())
    first, second = group_sums(s.stat2_rx)
    dz = (s.rstd[0:1, :] * (s.slope0[...] - first - s.z[...] * second)).astype(BF16)
    s.grad[...] = nn(s.patches_t[...], dz)

    def rows_at(k):
        return pl.ds(pl.multiple_of(k * taps, 8), taps)

    def grad_copy(p, source):
        return send(s.grad_tx.at[p], s.grad_rx.at[source], s.grad_sem, p, source, sp=p)

    def grad_out(p):
        s.grad_tx[p] = s.grad[rows_at(p), :].astype(BF16)
        grad_copy(p, me).start()

    others(n_sp, me, grad_out)
    s.grad_rx[me] = s.grad[rows_at(me), :].astype(BF16)

    others(n_dp, image, lambda p: down_out(p, p, p).wait_recv())

    def add_down(p):
        out_down[...] += s.gd_rx[p].astype(F32)

    others(n_dp, image, add_down)

    others(n_sp, me, lambda p: grad_copy(p, p).wait_recv())

    def slots(ref, n):
        total = ref[0].astype(F32)
        for j in range(1, n):
            total = total + ref[j].astype(F32)
        return total

    s.all_tx[...] = slots(s.grad_rx, n_sp).astype(BF16)
    s.all_rx[image] = s.all_tx[...]

    def all_copy(p, source):
        return send(s.all_tx, s.all_rx.at[source], s.all_sem, p, source, dp=p)

    others(n_dp, image, lambda p: all_copy(p, image).start())
    others(n_dp, image, lambda p: all_copy(p, p).wait_recv())
    s.last_tx[...] = slots(s.all_rx, n_dp).astype(BF16)
    s.last_rx[me] = s.last_tx[...]

    def last_copy(p, source):
        return send(s.last_tx, s.last_rx.at[source], s.last_sem, p, source, sp=p)

    others(n_sp, me, lambda p: last_copy(p, me).start())

    others(n_dp, image, lambda p: q_copy(p, p).wait_recv())
    others(n_dp, image, lambda p: side_copy(p, p).wait_recv())
    here = s.emb[:, pl.ds(pl.multiple_of(image * block, block), block)].astype(F32) - mean_col
    here_t = here.T
    s.emb_t[...] = here_t
    which = lax.broadcasted_iota(jnp.int32, (n_dp, block), 0)
    shifts = jnp.zeros((n_dp, block), F32)
    sums = jnp.zeros((n_dp, block), F32)
    for k in range(n_dp):
        shifts = jnp.where(which == k, s.side_rx[k, 1:2, :], shifts)
        sums = jnp.where(which == k, s.side_rx[k, 2:3, :], sums)
    out_up[...] = exact(shifts, sums, ((0,), (0,)))

    def up_part(k):
        left = here_t * s.side_rx[k].T[:, 0:1]
        out_up[...] += nn(left.astype(BF16), s.q_rx[k])

    for k in range(n_dp):
        up_part(k)

    others(n_sp, me, lambda p: last_copy(p, p).wait_recv())

    def show(k):
        out_conv[rows_at(k), :] = s.last_rx[k].astype(F32)

    every(n_sp, show)

    for copy in (mix_copy, off_copy, pair_copy, sum_copy):
        copy.wait_send()

    def left(p):
        for copy in (stat_copy(p), act_copy(p, me), part_copy(p, me), stat2_copy(p, me), grad_copy(p, me)):
            copy.wait_send()
        last_copy(p, me).wait_send()

    others(n_sp, me, left)

    def left_dp(p):
        for copy in (down_out(p, image, p), q_copy(p, image), side_copy(p, image), all_copy(p, image)):
            copy.wait_send()

    others(n_dp, image, left_dp)

    def left_block(p):
        sib_copy(p).wait_send()
        for name in routes:
            cot_copy(name, p).wait_send()

    every(n_dp, left_block)


class Scratch:
    def __init__(self, names, refs):
        for name, ref in zip(names, refs):
            setattr(self, name, ref)


def on_device(
    n_sp, n_dp, feats, conv_w, group_norm_gain, group_norm_bias, emb_w, time_w, up_w, down_w, steps, cotangent
):
    image = feats[0]
    rows_in, cols_in, in_chans = image.shape
    rows, cols = rows_in // 2, cols_in // 2
    rim = lax.ppermute(image[:, cols_in - 1, :], "sp", [(i, i + 1) for i in range(n_sp - 1)])
    widened = jnp.concatenate([rim[:, None, :], image], axis=1)
    padded = jnp.pad(widened, ((1, 0), (0, 0), (0, 0)))
    pieces = []
    for row_tap in range(3):
        for col_tap in range(3):
            pieces.append(padded[row_tap : row_tap + 2 * rows : 2, col_tap : col_tap + 2 * cols : 2, :])
    pixels = rows * cols
    patches = jnp.concatenate(pieces, axis=-1).reshape(pixels, 9 * in_chans)
    freq_count = time_w.shape[0] // 2
    freqs = jnp.exp(-math.log(10000.0) * jnp.arange(freq_count, dtype=F32) / freq_count)
    angle = steps[0].astype(F32) * freqs
    embed = jax.nn.silu(jnp.concatenate([jnp.cos(angle), jnp.sin(angle)])).astype(BF16)
    es = jnp.broadcast_to(embed[None, :], (16, embed.shape[0]))
    gain_bias = jnp.concatenate(
        [group_norm_gain[None], group_norm_bias[None], jnp.zeros((6, group_norm_gain.shape[0]), F32)]
    )
    chans = conv_w.shape[1]
    width = emb_w.shape[1]
    hidden = up_w.shape[1]
    block = width // n_dp
    n_chip = n_sp // 2
    taps = conv_w.shape[0] // n_sp
    half = pixels // 2
    tokens = n_chip * pixels
    vm = pltpu.VMEM
    dma = lambda n: pltpu.SemaphoreType.DMA((2, n))
    scratch = dict(
        load=pltpu.SemaphoreType.DMA((8 + 2 * n_dp,)),
        stat_sem=dma(n_sp), act_sem=dma(n_sp), part_sem=dma(n_sp), stat2_sem=dma(n_sp),
        grad_sem=dma(n_sp), last_sem=dma(n_sp), cot_sem=dma(9 * n_dp), pair_sem=dma(8),
        sib_sem=dma(n_dp), gd_sem=dma(n_dp), q_sem=dma(n_dp), side_sem=dma(n_dp), all_sem=dma(n_dp),
        patches=vm(patches.shape, BF16), conv=vm(conv_w.shape, BF16), emb=vm(emb_w.shape, BF16),
        time=vm((2, time_w.shape[0], 1024), BF16), up=vm(up_w.shape, BF16),
        gated=vm((n_dp, 2 * hidden, block), BF16), cot=vm((n_dp, n_chip, pixels, block), BF16),
        z=vm((pixels, chans), F32), slope0=vm((pixels, chans), F32), rstd=vm((8, chans), F32),
        stat_tx=vm((8, chans), F32), stat_rx=vm((n_sp, 8, chans), F32),
        stat2_tx=vm((8, chans), F32), stat2_rx=vm((n_sp, 8, chans), F32),
        mod=vm((16, 3 * width), F32), act_tx=vm((2, half, chans), BF16),
        act_rx=vm((n_sp, half, chans), BF16), act=vm((n_chip, pixels, chans), F32),
        act_t=vm((chans, tokens), BF16), mean_col=vm((chans, 128), F32), gram=vm((chans, chans), F32),
        gram_hi=vm((chans, chans), BF16), gram_lo=vm((chans, chans), BF16),
        mix=vm((chans, hidden), F32), mixer=vm((chans, 2 * hidden), BF16),
        offset=vm((16, hidden), F32), offsets=vm((16, 2 * hidden), F32), skip=vm((pixels, chans), F32),
        hid_t=vm((2 * hidden, tokens), BF16), slope=vm((n_chip, pixels, 2 * hidden), F32),
        moved=vm((n_chip, pixels, 2 * hidden), F32), dhid=vm((n_chip, pixels, 2 * hidden), F32),
        spread=vm((n_chip, pixels, chans), F32), token_rstd=vm((n_chip, pixels, 128), F32),
        patches_t=vm((patches.shape[1], pixels), BF16),
        sib_tx=vm((n_dp, hidden, block), BF16), sib_rx=vm((n_dp, hidden, block), BF16),
        gd_own=vm((2, hidden, block), F32), gd_tx=vm((n_dp, hidden, block), BF16),
        gd_rx=vm((n_dp, hidden, block), BF16), du_sum=vm((8, 2 * hidden), F32),
        du=vm((tokens, 2 * hidden), BF16), part_tx=vm((n_sp, half, chans), BF16),
        part_rx=vm((n_sp, half, chans), BF16), pairs=vm((chans, 2 * hidden), F32),
        pair_tx=vm((chans, hidden), BF16), pair_rx=vm((chans, hidden), BF16),
        sum_tx=vm((8, hidden), F32), sum_rx=vm((8, hidden), F32), q_tx=vm((chans, hidden), BF16),
        q_rx=vm((n_dp, chans, hidden), BF16), side_tx=vm((n_dp, 8, block), F32),
        side_rx=vm((n_dp, 8, block), F32), grad=vm((conv_w.shape[0], chans), F32),
        grad_tx=vm((n_sp, taps, chans), BF16), grad_rx=vm((n_sp, taps, chans), BF16),
        all_tx=vm((taps, chans), BF16), all_rx=vm((n_dp, taps, chans), BF16),
        last_tx=vm((taps, chans), BF16), last_rx=vm((n_sp, taps, chans), BF16),
        emb_t=vm((block, chans), F32),
    )
    names = tuple(scratch)

    def kernel(*refs):
        body(n_sp, n_dp, *refs[:12], Scratch(names, refs[12:]))

    in_vmem = pl.BlockSpec(memory_space=pltpu.VMEM)
    in_place = pl.BlockSpec(memory_space=pl.ANY)
    return pl.pallas_call(
        kernel,
        out_shape=(
            jax.ShapeDtypeStruct(conv_w.shape, F32),
            jax.ShapeDtypeStruct((block, hidden), F32),
            jax.ShapeDtypeStruct((hidden, block), F32),
        ),
        in_specs=[in_vmem] * 2 + [in_place] * 7,
        out_specs=(in_vmem,) * 3,
        scratch_shapes=list(scratch.values()),
        compiler_params=pltpu.CompilerParams(
            collective_id=0, has_side_effects=True, vmem_limit_bytes=67043328
        ),
    )(es, gain_bias, patches, conv_w, emb_w, time_w, up_w, down_w, cotangent[0])


def solution(mesh):
    in_specs = (
        P("dp", None, "sp", None),
        P(),
        P(),
        P(),
        P(),
        P(),
        P(None, "sp"),
        P("sp", None),
        P("dp"),
        P("dp", "sp", None),
    )
    out_specs = (P(), P("dp", "sp"), P("sp", "dp"))
    return jax.shard_map(
        functools.partial(on_device, mesh.shape["sp"], mesh.shape["dp"]),
        mesh=mesh,
        in_specs=in_specs,
        out_specs=out_specs,
        check_vma=False,
    )
```

```python
import functools
import math

import jax
import jax.numpy as jnp
from jax import lax
from jax.experimental import pallas as pl
from jax.experimental.pallas import tpu as pltpu
from jax.sharding import PartitionSpec as P

NORM_GROUPS = 32
F32 = jnp.float32
BF16 = jnp.bfloat16
MESH = pl.DeviceIdType.MESH


def gelu_pair(u):
    coef = math.sqrt(2.0 / math.pi)
    inner = coef * (u + 0.044715 * u * u * u)
    tangent = jnp.tanh(inner)
    value = 0.5 * u * (1.0 + tangent)
    slope = 0.5 * (1.0 + tangent) + 0.5 * u * (1.0 - tangent * tangent) * coef * (
        1.0 + 3.0 * 0.044715 * u * u
    )
    return (value, slope)


def nn(left, right):
    return lax.dot_general(left, right, (((1,), (0,)), ((), ())), preferred_element_type=F32)


def nt(left, right):
    return lax.dot_general(left, right, (((1,), (1,)), ((), ())), preferred_element_type=F32)


def exact(left, right, dims):
    return lax.dot_general(
        left,
        right,
        (dims, ((), ())),
        precision=lax.Precision.HIGHEST,
        preferred_element_type=F32,
    )


def split(value):
    high = value.astype(BF16)
    return high, (value - high.astype(F32)).astype(BF16)


def rows_of(first, second, like):
    which = lax.broadcasted_iota(jnp.int32, like, 0)
    return jnp.where(which == 0, first, jnp.where(which == 1, second, 0.0))


def body(
    n_sp, n_dp, es, gain, bias, planes, conv_in, emb_in, time_in, up_in, down_in, cot_in,
    out_conv, out_up, out_down, s,
):
    n_chip = n_sp // 2
    width = emb_in.shape[1]
    hidden = up_in.shape[1]
    block = width // n_dp
    chans = conv_in.shape[1]
    rows, cols, in_chans = planes.shape[2:]
    pixels = rows * cols
    half = pixels // 2
    taps = conv_in.shape[0] // n_sp
    me = lax.axis_index("sp")
    image = lax.axis_index("dp")
    core = lax.rem(me, 2)
    chip = me // 2
    far = lax.rem(chip, 2)
    col = chip // 2
    n_col = n_chip // 2
    east_col, west_col = lax.rem(col + 1, n_col), lax.rem(col + n_col - 1, n_col)
    over_col = lax.rem(col + 2, n_col)
    sibling = chip * 2 + 1 - core
    chip_of = lambda at, level: at * 2 + level
    dev_of = lambda which: which * 2 + core
    z_chip = chip_of(col, 1 - far)
    east, west = dev_of(chip_of(east_col, far)), dev_of(chip_of(west_col, far))
    z_peer = dev_of(z_chip)

    def send(src, dst, sems, at_send, at_recv, **where):
        return pltpu.make_async_remote_copy(
            src_ref=src, dst_ref=dst, send_sem=sems.at[0, at_send], recv_sem=sems.at[1, at_recv],
            device_id=where, device_id_type=MESH,
        )

    def others(count, first, act):
        @pl.loop(1, count)
        def _(step):
            act(lax.rem(first + step, count))

    def every(count, act):
        @pl.loop(0, count)
        def _(step):
            act(step)

    barrier = pltpu.get_barrier_semaphore()
    others(n_sp, me, lambda p: pl.semaphore_signal(barrier, 1, device_id={"sp": p}, device_id_type=MESH))
    others(n_dp, image, lambda p: pl.semaphore_signal(barrier, 1, device_id={"dp": p}, device_id_type=MESH))

    loads = {}
    for index, (name, src, dst) in enumerate(
        (
            ("conv", conv_in, s.conv),
            ("emb", emb_in, s.emb),
            ("up", up_in, s.up),
        )
    ):
        loads[name] = pltpu.make_async_copy(src, dst, s.load.at[index])

    def cot_load(p):
        columns = pl.ds(pl.multiple_of(p * block, block), block)
        return pltpu.make_async_copy(cot_in.at[:, columns], s.cot.at[p, chip], s.load.at[8 + p])

    my_rows = pl.ds(pl.multiple_of(core * hidden, hidden), hidden)
    its_rows = pl.ds(pl.multiple_of((1 - core) * hidden, hidden), hidden)

    def down_load(p):
        columns = pl.ds(pl.multiple_of(p * block, block), block)
        return pltpu.make_async_copy(
            down_in.at[:, columns], s.gated.at[p, my_rows], s.load.at[8 + n_dp + p]
        )

    def time_load(k):
        columns = pl.ds(pl.multiple_of(k * 1024, 1024), 1024)
        return pltpu.make_async_copy(time_in.at[:, columns], s.time.at[k], s.load.at[8 + 2 * n_dp + k])

    n_time = 3 * width // 1024

    loads["conv"].start()
    every(n_dp, lambda p: cot_load(p).start())
    every(n_dp, lambda p: down_load(p).start())
    every(n_time, lambda k: time_load(k).start())
    for name in ("emb", "up"):
        loads[name].start()

    for parity in range(2):
        s.rim_tx[parity] = planes[parity, 1].astype(F32)[:, cols - 1, :].astype(BF16)

    @pl.when(me == 0)
    def _():
        s.rim_rx[...] = jnp.zeros_like(s.rim_rx)

    pl.semaphore_wait(barrier, n_sp - 1 + n_dp - 1)
    rim_copy = send(s.rim_tx, s.rim_rx, s.pair_sem, 5, 5, sp=lax.rem(me + 1, n_sp))

    @pl.when(me < n_sp - 1)
    def _():
        rim_copy.start()

    first_column = lax.broadcasted_iota(jnp.int32, (rows, cols, in_chans), 1) == 0

    def patch(row_tap, col_tap):
        parity = (row_tap + 1) % 2
        value = planes[parity, (col_tap + 1) % 2].astype(F32)
        if col_tap == 0:
            value = pltpu.roll(value, 1, 1)
            value = jnp.where(first_column, s.rim_rx[parity].astype(F32)[:, None, :], value)
        if row_tap == 0:
            value = jnp.concatenate([jnp.zeros_like(value[:1]), value[:-1]], axis=0)
        tap = row_tap * 3 + col_tap
        s.patches[:, tap * in_chans : (tap + 1) * in_chans] = value.reshape(pixels, in_chans).astype(BF16)

    for row_tap in range(3):
        for col_tap in (1, 2):
            patch(row_tap, col_tap)
    loads["conv"].wait()

    @pl.when(me > 0)
    def _():
        rim_copy.wait_recv()

    for row_tap in range(3):
        patch(row_tap, 0)
    s.z[...] = nn(s.patches[...], s.conv[...])
    z = s.z[...]
    s.stat_tx[...] = rows_of(
        jnp.sum(z, axis=0, keepdims=True), jnp.sum(z * z, axis=0, keepdims=True), (8, chans)
    )
    s.stat_rx[me] = s.stat_tx[...]

    def stat_copy(p):
        return send(s.stat_tx, s.stat_rx.at[me], s.stat_sem, p, me, sp=p)

    def stat_from(p):
        return send(s.stat_tx, s.stat_rx.at[p], s.stat_sem, p, p, sp=p)

    others(n_sp, me, lambda p: stat_copy(p).start())

    every(n_dp, lambda p: cot_load(p).wait())

    def turn(q):
        return lax.rem(image + 1 + q, n_dp)

    top, low = pl.ds(0, half), pl.ds(half, half)
    routes = {
        "z": (chip, None, z_peer, z_chip),
        "e": (chip, None, east, chip_of(west_col, far)),
        "w": (chip, None, west, chip_of(east_col, far)),
        "ez": (z_chip, None, east, chip_of(west_col, 1 - far)),
        "wz": (z_chip, None, west, chip_of(east_col, 1 - far)),
        "ee": (chip_of(west_col, far), top, east, chip_of(over_col, far)),
        "ww": (chip_of(east_col, far), low, west, chip_of(over_col, far)),
        "eez": (chip_of(west_col, 1 - far), top, east, chip_of(over_col, 1 - far)),
        "wwz": (chip_of(east_col, 1 - far), low, west, chip_of(over_col, 1 - far)),
    }
    order = {name: index for index, name in enumerate(routes)}

    def cot_copy(name, p, arriving=False):
        mine, part, to, theirs = routes[name]
        which = theirs if arriving else mine
        ref = s.cot.at[p, which] if part is None else s.cot.at[p, which, part, :]
        at = order[name] * n_dp + p
        return send(ref, ref, s.cot_sem, at, at, sp=to)

    def own(q):
        p = turn(q)
        for name in ("z", "e", "w"):
            cot_copy(name, p).start()

    def relay(q, steps):
        p = turn(q)
        for name, then in steps:
            cot_copy(name, p, True).wait_recv()
            for onward in then:
                cot_copy(onward, p).start()

    def relay_near(q):
        relay(q, (("z", ("ez", "wz")), ("e", ("ee",)), ("w", ("ww",))))

    def relay_far(q):
        relay(q, (("ez", ("eez",)), ("wz", ("wwz",))))

    def landed(q):
        p = turn(q)
        for name in ("ee", "ww", "eez", "wwz"):
            cot_copy(name, p, True).wait_recv()

    own(0)
    own(1)

    every(n_dp, lambda p: down_load(p).wait())
    my_down, its_down = s.gated.at[:, my_rows], s.gated.at[:, its_rows]
    down_copy = send(my_down, my_down, s.pair_sem, 0, 0, sp=sibling)
    down_copy.start()

    def mod_part(k):
        columns = pl.ds(pl.multiple_of(k * 1024, 1024), 1024)
        time_load(k).wait()
        s.mod[:, columns] = nn(es[...], s.time[k])

    every(n_time, mod_part)

    others(n_sp, me, lambda p: stat_from(p).wait_recv())
    count = pixels * n_sp * (chans // NORM_GROUPS)
    shift_by = (chans // NORM_GROUPS).bit_length() - 1

    def group_sums(ref):
        pair = lax.broadcasted_iota(jnp.int32, (chans, chans), 0) >> shift_by
        other = lax.broadcasted_iota(jnp.int32, (chans, chans), 1) >> shift_by
        same = jnp.where(pair == other, 1.0, 0.0).astype(F32)
        totals = exact(jnp.sum(ref[...], axis=0), same, ((1,), (0,))) / count
        return totals[0:1, :], totals[1:2, :]

    mean, square = group_sums(s.stat_rx)
    rstd = lax.rsqrt(square - mean * mean + 1e-05)
    s.rstd[...] = jnp.broadcast_to(rstd, s.rstd.shape)
    xhat = (s.z[...] - mean) * rstd
    s.z[...] = xhat
    pre = xhat * gain[...] + bias[...]
    sigma = jax.nn.sigmoid(pre)
    s.slope0[...] = sigma * (1.0 + pre * (1.0 - sigma)) * gain[...]
    act = (pre * sigma).reshape(n_chip, 2, pixels // n_sp, chans)
    for k in range(2):
        s.act_tx[k] = act[:, k].reshape(half, chans).astype(BF16)
    s.act_rx[me] = s.act_tx[core]

    def act_copy(p, source):
        return send(s.act_tx.at[lax.rem(p, 2)], s.act_rx.at[source], s.act_sem, p, source, sp=p)

    others(n_sp, me, lambda p: act_copy(p, me).start())
    own(2)
    relay_near(0)
    own(3)

    loads["emb"].wait()
    loads["up"].wait()
    ones = jnp.ones((16, width), BF16)
    mean_row = nt(ones, s.emb[...])[0:1, :] / width
    s.mean_col[...] = jnp.broadcast_to(
        jnp.mean(s.emb[...].astype(F32), axis=1, keepdims=True), s.mean_col.shape
    )
    mean_col = s.mean_col[:, 0:1]
    s.gram[...] = jnp.zeros_like(s.gram)
    s.mix[...] = jnp.zeros_like(s.mix)
    s.offset[...] = jnp.zeros_like(s.offset)
    s.skip[...] = jnp.zeros_like(s.skip)

    def fold(p):
        columns = pl.ds(pl.multiple_of(p * block, block), block)
        emb = s.emb[:, columns]
        scale = s.mod[0:1, pl.ds(pl.multiple_of(width + p * block, block), block)]
        left = ((emb.astype(F32) - mean_col) * (1.0 + scale)).astype(BF16)
        up = s.up[columns, :]
        s.mix[...] += nn(left, up)
        s.gram[...] += nt(emb, emb)
        high, low_part = split(s.mod[:, columns])
        s.offset[...] += nn(high, up) + nn(low_part, up)
        s.skip[...] += nt(s.cot[p, chip], emb)

    every(n_dp, fold)
    my_cols, its_cols = my_rows, its_rows
    s.mixer[:, my_cols] = s.mix[...].astype(BF16)
    s.offsets[:, my_cols] = s.offset[...]
    mix_copy = send(s.mixer.at[:, my_cols], s.mixer.at[:, my_cols], s.pair_sem, 1, 1, sp=sibling)
    mix_copy.start()
    off_copy = send(s.offsets.at[:, my_cols], s.offsets.at[:, my_cols], s.pair_sem, 2, 2, sp=sibling)
    off_copy.start()
    relay_near(1)
    relay_far(0)
    own(4)

    down_from = send(its_down, its_down, s.pair_sem, 0, 0, sp=sibling)
    down_copy.wait_send()
    down_from.wait_recv()

    def gate_part(p):
        gate = s.mod[0:1, pl.ds(pl.multiple_of(2 * width + p * block, block), block)]
        s.gated[p] = (s.gated[p].astype(F32) * gate).astype(BF16)

    every(n_dp, gate_part)

    others(n_sp, me, lambda p: act_copy(p, p).wait_recv())

    def place(p):
        tile = s.act_rx[p].astype(F32).reshape(n_chip, pixels // n_sp, chans)
        s.act[:, pl.ds(pl.multiple_of(p * 8, 8), 8), :] = tile

    every(n_sp, place)
    mix_from = send(s.mixer.at[:, its_cols], s.mixer.at[:, its_cols], s.pair_sem, 1, 1, sp=sibling)
    off_from = send(s.offsets.at[:, its_cols], s.offsets.at[:, its_cols], s.pair_sem, 2, 2, sp=sibling)
    mix_from.wait_recv()
    off_from.wait_recv()
    gram_hi, gram_lo = split(s.gram[...] - width * mean_col * mean_row)
    s.gram_hi[...] = gram_hi
    s.gram_lo[...] = gram_lo

    def forward(i):
        lanes = pl.ds(pl.multiple_of(i * pixels, pixels), pixels)
        wide = s.act[i]
        narrow = wide.astype(BF16)
        spread = nn(narrow, s.gram_hi[...]) + nn(narrow, s.gram_lo[...])
        var = jnp.sum(wide * spread, axis=-1, keepdims=True) / width
        token_rstd = lax.rsqrt(var + 1e-06)
        moved = nn(narrow, s.mixer[...]) * token_rstd
        value, slope = gelu_pair(moved + s.offsets[0:1, :])
        s.hid_t[:, lanes] = value.T.astype(BF16)
        s.act_t[:, lanes] = wide.T.astype(BF16)
        s.slope[i] = slope
        s.moved[i] = moved
        s.spread[i] = spread * (token_rstd / width)
        s.token_rstd[i] = jnp.broadcast_to(token_rstd, (pixels, 128))
        s.dhid[i] = jnp.zeros_like(slope)

    relay_near(2)
    relay_far(1)
    every(n_chip, forward)
    s.patches_t[...] = s.patches[...].astype(F32).T.astype(BF16)

    def sib_copy(p):
        return send(s.sib_tx.at[p], s.sib_rx.at[p], s.sib_sem, p, p, sp=sibling)

    def down_out(p, source, to):
        return send(s.gd_tx.at[p], s.gd_rx.at[source], s.gd_sem, p, source, dp=to)

    def block_of(q):
        p = turn(q)
        gate = s.mod[0:1, pl.ds(pl.multiple_of(2 * width + p * block, block), block)]
        cot = s.cot[p].reshape(n_chip * pixels, block)
        s.sib_tx[p] = (nn(s.hid_t[its_rows, :], cot) * gate).astype(BF16)
        sib_copy(p).start()
        s.gd_own[lax.rem(q, 2)] = nn(s.hid_t[my_rows, :], cot) * gate

        def part(h):
            rows = pl.ds(h * (n_chip // 2), n_chip // 2)
            tokens = s.cot[p, rows].reshape(n_chip // 2 * pixels, block)
            s.dhid[rows] += nt(tokens, s.gated[p]).reshape(n_chip // 2, pixels, 2 * hidden)

        every(2, part)

    def whole(q):
        p = turn(q)
        sib_copy(p).wait_recv()
        return p, s.gd_own[lax.rem(q, 2)] + s.sib_rx[p].astype(F32)

    def hand_over(q):
        p, total = whole(q)
        s.gd_tx[p] = total.astype(BF16)
        down_out(p, image, p).start()

    @pl.loop(0, n_dp)
    def _(q):
        @pl.when(q + 5 < n_dp)
        def _():
            own(q + 5)

        @pl.when(q + 3 < n_dp)
        def _():
            relay_near(q + 3)

        @pl.when(q + 2 < n_dp)
        def _():
            relay_far(q + 2)

        @pl.when(q > 0)
        def _():
            hand_over(q - 1)

        landed(q)
        block_of(q)

    s.du_sum[...] = jnp.zeros_like(s.du_sum)

    def backward(i):
        grad = s.dhid[i] * s.slope[i]
        s.du_sum[0:1, :] += jnp.sum(grad, axis=0, keepdims=True)
        grad = grad * s.token_rstd[i][:, 0:1]
        cross = jnp.sum(grad * s.moved[i], axis=-1, keepdims=True)
        narrow = grad.astype(BF16)
        s.du[pl.ds(pl.multiple_of(i * pixels, pixels), pixels), :] = narrow
        s.act[i] = nt(narrow, s.mixer[...]) - cross * s.spread[i]

    every(n_chip, backward)
    s.act[chip] += s.skip[...]

    def tile_of(p):
        rows = s.act[:, pl.ds(pl.multiple_of(p * 8, 8), 8), :]
        return rows.reshape(half, chans).astype(BF16)

    def part_copy(p, source):
        return send(s.part_tx.at[p], s.part_rx.at[source], s.part_sem, p, source, sp=p)

    def part_out(p):
        s.part_tx[p] = tile_of(p)
        part_copy(p, me).start()

    others(n_sp, me, part_out)
    s.part_rx[me] = tile_of(me)

    s.pairs[...] = nn(s.act_t[...], s.du[...])
    s.pair_tx[...] = s.pairs[:, its_cols].astype(BF16)
    s.sum_tx[...] = s.du_sum[:, its_cols]
    pair_copy = send(s.pair_tx, s.pair_rx, s.pair_sem, 3, 3, sp=sibling)
    pair_copy.start()
    sum_copy = send(s.sum_tx, s.sum_rx, s.pair_sem, 4, 4, sp=sibling)
    sum_copy.start()
    _, total = whole(n_dp - 1)
    out_down[...] = total

    pair_copy.wait_recv()
    sum_copy.wait_recv()
    s.q_tx[...] = (s.pairs[:, my_cols] + s.pair_rx[...].astype(F32)).astype(BF16)
    s.q_rx[image] = s.q_tx[...]
    du_sum = (s.du_sum[:, my_cols] + s.sum_rx[...])[0:1, :]

    def side_of(p):
        shift = s.mod[0:1, pl.ds(pl.multiple_of(p * block, block), block)]
        scale = s.mod[0:1, pl.ds(pl.multiple_of(width + p * block, block), block)]
        which = lax.broadcasted_iota(jnp.int32, (8, block), 0)
        return jnp.where(which == 2, du_sum, rows_of(1.0 + scale, shift, (8, block)))

    def q_copy(p, source):
        return send(s.q_tx, s.q_rx.at[source], s.q_sem, p, source, dp=p)

    def side_copy(p, source):
        return send(s.side_tx.at[p], s.side_rx.at[source], s.side_sem, p, source, dp=p)

    n_row = n_dp // 2
    row_first = image // n_row * n_row
    twin = lax.rem(image + n_row, n_dp)

    def in_row(act):
        others(n_row, image - row_first, lambda at: act(row_first + at))

    def forward_copy(p):
        at = lax.rem(p + n_row, n_dp)
        return send(s.q_rx.at[twin], s.q_rx.at[twin], s.q_sem, at, twin, dp=p)

    def side_out(p):
        s.side_tx[p] = side_of(p)
        side_copy(p, image).start()

    q_copy(twin, image).start()
    in_row(lambda p: q_copy(p, image).start())
    others(n_dp, image, side_out)
    s.side_rx[image] = side_of(image)

    others(n_sp, me, lambda p: part_copy(p, p).wait_recv())
    parts = []
    for k in range(2):
        total = s.part_rx[k].astype(F32)
        for j in range(1, n_chip):
            total = total + s.part_rx[2 * j + k].astype(F32)
        parts.append(total.reshape(n_chip, 1, pixels // n_sp, chans))
    dx = jnp.concatenate(parts, axis=1).reshape(pixels, chans) * s.slope0[...]
    s.slope0[...] = dx
    s.stat2_tx[...] = rows_of(
        jnp.sum(dx, axis=0, keepdims=True), jnp.sum(dx * s.z[...], axis=0, keepdims=True), (8, chans)
    )
    s.stat2_rx[me] = s.stat2_tx[...]

    def stat2_copy(p, source):
        return send(s.stat2_tx, s.stat2_rx.at[source], s.stat2_sem, p, source, sp=p)

    others(n_sp, me, lambda p: stat2_copy(p, me).start())

    others(n_sp, me, lambda p: stat2_copy(p, p).wait_recv())
    first, second = group_sums(s.stat2_rx)
    dz = (s.rstd[0:1, :] * (s.slope0[...] - first - s.z[...] * second)).astype(BF16)
    s.grad[...] = nn(s.patches_t[...], dz)

    def rows_at(k):
        return pl.ds(pl.multiple_of(k * taps, 8), taps)

    n_half = 2
    lanes_of = lambda h: slice(h * (chans // n_half), (h + 1) * (chans // n_half))

    def grad_copy(h, p, source):
        at = h * n_sp
        return send(s.grad_tx.at[h, p], s.grad_rx.at[h, source], s.grad_sem, at + p, at + source, sp=p)

    def all_copy(h, p, source):
        at = h * n_dp
        return send(s.all_tx.at[h], s.all_rx.at[h, source], s.all_sem, at + p, at + source, dp=p)

    def last_copy(h, p, source):
        at = h * n_sp
        return send(s.last_tx.at[h], s.last_rx.at[h, source], s.last_sem, at + p, at + source, sp=p)

    for h in range(n_half):

        def grad_out(p, h=h):
            s.grad_tx[h, p] = s.grad[rows_at(p), lanes_of(h)].astype(BF16)
            grad_copy(h, p, me).start()

        others(n_sp, me, grad_out)
        s.grad_rx[h, me] = s.grad[rows_at(me), lanes_of(h)].astype(BF16)

    def slots(ref, h, n):
        total = ref[h, 0].astype(F32)
        for j in range(1, n):
            total = total + ref[h, j].astype(F32)
        return total

    for h in range(n_half):
        others(n_sp, me, lambda p: grad_copy(h, p, p).wait_recv())
        s.all_tx[h] = slots(s.grad_rx, h, n_sp).astype(BF16)
        s.all_rx[h, image] = s.all_tx[h]
        others(n_dp, image, lambda p: all_copy(h, p, image).start())

    q_copy(twin, twin).wait_recv()
    in_row(lambda p: forward_copy(p).start())

    for h in range(n_half):
        others(n_dp, image, lambda p: all_copy(h, p, p).wait_recv())
        s.last_tx[h] = slots(s.all_rx, h, n_dp).astype(BF16)
        s.last_rx[h, me] = s.last_tx[h]
        others(n_sp, me, lambda p: last_copy(h, p, me).start())

    others(n_dp, image, lambda p: down_out(p, p, p).wait_recv())

    def add_down(p):
        out_down[...] += s.gd_rx[p].astype(F32)

    others(n_dp, image, add_down)

    in_row(lambda p: q_copy(p, p).wait_recv())
    in_row(lambda p: q_copy(p, lax.rem(p + n_row, n_dp)).wait_recv())
    others(n_dp, image, lambda p: side_copy(p, p).wait_recv())
    here = s.emb[:, pl.ds(pl.multiple_of(image * block, block), block)].astype(F32) - mean_col
    here_t = here.T
    s.emb_t[...] = here_t
    which = lax.broadcasted_iota(jnp.int32, (n_dp, block), 0)
    shifts = jnp.zeros((n_dp, block), F32)
    sums = jnp.zeros((n_dp, block), F32)
    for k in range(n_dp):
        shifts = jnp.where(which == k, s.side_rx[k, 1:2, :], shifts)
        sums = jnp.where(which == k, s.side_rx[k, 2:3, :], sums)
    out_up[...] = exact(shifts, sums, ((0,), (0,)))

    def up_part(k):
        left = here_t * s.side_rx[k].T[:, 0:1]
        out_up[...] += nn(left.astype(BF16), s.q_rx[k])

    for k in range(n_dp):
        up_part(k)

    for h in range(n_half):
        others(n_sp, me, lambda p: last_copy(h, p, p).wait_recv())

        def show(k, h=h):
            out_conv[rows_at(k), lanes_of(h)] = s.last_rx[h, k].astype(F32)

        every(n_sp, show)

    for copy in (mix_copy, off_copy, pair_copy, sum_copy):
        copy.wait_send()

    @pl.when(me < n_sp - 1)
    def _():
        rim_copy.wait_send()

    def left(p):
        for copy in (stat_copy(p), act_copy(p, me), part_copy(p, me), stat2_copy(p, me)):
            copy.wait_send()
        for h in range(n_half):
            grad_copy(h, p, me).wait_send()
            last_copy(h, p, me).wait_send()

    others(n_sp, me, left)

    def left_dp(p):
        for copy in (down_out(p, image, p), q_copy(p, image), side_copy(p, image)):
            copy.wait_send()
        for h in range(n_half):
            all_copy(h, p, image).wait_send()

    others(n_dp, image, left_dp)

    def left_block(p):
        sib_copy(p).wait_send()
        for name in routes:
            cot_copy(name, p).wait_send()

    every(n_dp, left_block)


class Scratch:
    def __init__(self, names, refs):
        for name, ref in zip(names, refs):
            setattr(self, name, ref)


def on_device(
    n_sp, n_dp, feats, conv_w, group_norm_gain, group_norm_bias, emb_w, time_w, up_w, down_w, steps, cotangent
):
    image = feats[0]
    rows_in, cols_in, in_chans = image.shape
    rows, cols = rows_in // 2, cols_in // 2
    pixels = rows * cols
    planes = image.reshape(rows, 2, cols, 2, in_chans).transpose(1, 3, 0, 2, 4)
    freq_count = time_w.shape[0] // 2
    freqs = jnp.exp(-math.log(10000.0) * jnp.arange(freq_count, dtype=F32) / freq_count)
    angle = steps[0].astype(F32) * freqs
    embed = jax.nn.silu(jnp.concatenate([jnp.cos(angle), jnp.sin(angle)])).astype(BF16)
    es = jnp.broadcast_to(embed[None, :], (16, embed.shape[0]))
    chans = conv_w.shape[1]
    width = emb_w.shape[1]
    hidden = up_w.shape[1]
    block = width // n_dp
    n_chip = n_sp // 2
    taps = conv_w.shape[0] // n_sp
    half = pixels // 2
    tokens = n_chip * pixels
    vm = pltpu.VMEM
    dma = lambda n: pltpu.SemaphoreType.DMA((2, n))
    scratch = dict(
        load=pltpu.SemaphoreType.DMA((8 + 2 * n_dp + time_w.shape[1] // 1024,)),
        stat_sem=dma(n_sp), act_sem=dma(n_sp), part_sem=dma(n_sp), stat2_sem=dma(n_sp),
        grad_sem=dma(2 * n_sp), last_sem=dma(2 * n_sp), cot_sem=dma(9 * n_dp), pair_sem=dma(8),
        sib_sem=dma(n_dp), gd_sem=dma(n_dp), q_sem=dma(n_dp), side_sem=dma(n_dp), all_sem=dma(2 * n_dp),
        patches=vm((pixels, 9 * in_chans), BF16), rim_tx=vm((2, rows, in_chans), BF16),
        rim_rx=vm((2, rows, in_chans), BF16), conv=vm(conv_w.shape, BF16), emb=vm(emb_w.shape, BF16),
        time=vm((time_w.shape[1] // 1024, time_w.shape[0], 1024), BF16), up=vm(up_w.shape, BF16),
        gated=vm((n_dp, 2 * hidden, block), BF16), cot=vm((n_dp, n_chip, pixels, block), BF16),
        z=vm((pixels, chans), F32), slope0=vm((pixels, chans), F32), rstd=vm((8, chans), F32),
        stat_tx=vm((8, chans), F32), stat_rx=vm((n_sp, 8, chans), F32),
        stat2_tx=vm((8, chans), F32), stat2_rx=vm((n_sp, 8, chans), F32),
        mod=vm((16, 3 * width), F32), act_tx=vm((2, half, chans), BF16),
        act_rx=vm((n_sp, half, chans), BF16), act=vm((n_chip, pixels, chans), F32),
        act_t=vm((chans, tokens), BF16), mean_col=vm((chans, 128), F32), gram=vm((chans, chans), F32),
        gram_hi=vm((chans, chans), BF16), gram_lo=vm((chans, chans), BF16),
        mix=vm((chans, hidden), F32), mixer=vm((chans, 2 * hidden), BF16),
        offset=vm((16, hidden), F32), offsets=vm((16, 2 * hidden), F32), skip=vm((pixels, chans), F32),
        hid_t=vm((2 * hidden, tokens), BF16), slope=vm((n_chip, pixels, 2 * hidden), F32),
        moved=vm((n_chip, pixels, 2 * hidden), F32), dhid=vm((n_chip, pixels, 2 * hidden), F32),
        spread=vm((n_chip, pixels, chans), F32), token_rstd=vm((n_chip, pixels, 128), F32),
        patches_t=vm((9 * in_chans, pixels), BF16),
        sib_tx=vm((n_dp, hidden, block), BF16), sib_rx=vm((n_dp, hidden, block), BF16),
        gd_own=vm((2, hidden, block), F32), gd_tx=vm((n_dp, hidden, block), BF16),
        gd_rx=vm((n_dp, hidden, block), BF16), du_sum=vm((8, 2 * hidden), F32),
        du=vm((tokens, 2 * hidden), BF16), part_tx=vm((n_sp, half, chans), BF16),
        part_rx=vm((n_sp, half, chans), BF16), pairs=vm((chans, 2 * hidden), F32),
        pair_tx=vm((chans, hidden), BF16), pair_rx=vm((chans, hidden), BF16),
        sum_tx=vm((8, hidden), F32), sum_rx=vm((8, hidden), F32), q_tx=vm((chans, hidden), BF16),
        q_rx=vm((n_dp, chans, hidden), BF16), side_tx=vm((n_dp, 8, block), F32),
        side_rx=vm((n_dp, 8, block), F32), grad=vm((conv_w.shape[0], chans), F32),
        grad_tx=vm((2, n_sp, taps, chans // 2), BF16), grad_rx=vm((2, n_sp, taps, chans // 2), BF16),
        all_tx=vm((2, taps, chans // 2), BF16), all_rx=vm((2, n_dp, taps, chans // 2), BF16),
        last_tx=vm((2, taps, chans // 2), BF16), last_rx=vm((2, n_sp, taps, chans // 2), BF16),
        emb_t=vm((block, chans), F32),
    )
    names = tuple(scratch)

    def kernel(*refs):
        body(n_sp, n_dp, *refs[:13], Scratch(names, refs[13:]))

    in_vmem = pl.BlockSpec(memory_space=pltpu.VMEM)
    in_place = pl.BlockSpec(memory_space=pl.ANY)
    return pl.pallas_call(
        kernel,
        out_shape=(
            jax.ShapeDtypeStruct(conv_w.shape, F32),
            jax.ShapeDtypeStruct((block, hidden), F32),
            jax.ShapeDtypeStruct((hidden, block), F32),
        ),
        in_specs=[in_vmem] * 4 + [in_place] * 6,
        out_specs=(in_vmem,) * 3,
        scratch_shapes=list(scratch.values()),
        compiler_params=pltpu.CompilerParams(
            collective_id=0, has_side_effects=True, vmem_limit_bytes=67043328
        ),
    )(es, group_norm_gain[None], group_norm_bias[None], planes, conv_w, emb_w, time_w, up_w, down_w, cotangent[0])


def solution(mesh):
    in_specs = (
        P("dp", None, "sp", None),
        P(),
        P(),
        P(),
        P(),
        P(),
        P(None, "sp"),
        P("sp", None),
        P("dp"),
        P("dp", "sp", None),
    )
    out_specs = (P(), P("dp", "sp"), P("sp", "dp"))
    return jax.shard_map(
        functools.partial(on_device, mesh.shape["sp"], mesh.shape["dp"]),
        mesh=mesh,
        in_specs=in_specs,
        out_specs=out_specs,
        check_vma=False,
    )
```

```python
import functools
import math

import jax
import jax.numpy as jnp
from jax import lax
from jax.experimental import pallas as pl
from jax.experimental.pallas import tpu as pltpu
from jax.sharding import PartitionSpec as P

NORM_GROUPS = 32
F32 = jnp.float32
BF16 = jnp.bfloat16
MESH = pl.DeviceIdType.MESH


def gelu_pair(u):
    coef = math.sqrt(2.0 / math.pi)
    inner = coef * (u + 0.044715 * u * u * u)
    tangent = jnp.tanh(inner)
    value = 0.5 * u * (1.0 + tangent)
    slope = 0.5 * (1.0 + tangent) + 0.5 * u * (1.0 - tangent * tangent) * coef * (
        1.0 + 3.0 * 0.044715 * u * u
    )
    return (value, slope)


def nn(left, right):
    return lax.dot_general(left, right, (((1,), (0,)), ((), ())), preferred_element_type=F32)


def nt(left, right):
    return lax.dot_general(left, right, (((1,), (1,)), ((), ())), preferred_element_type=F32)


def exact(left, right, dims):
    return lax.dot_general(
        left,
        right,
        (dims, ((), ())),
        precision=lax.Precision.HIGHEST,
        preferred_element_type=F32,
    )


def split(value):
    high = value.astype(BF16)
    return high, (value - high.astype(F32)).astype(BF16)


def rows_of(first, second, like):
    which = lax.broadcasted_iota(jnp.int32, like, 0)
    return jnp.where(which == 0, first, jnp.where(which == 1, second, 0.0))


def body(
    n_sp, n_dp, es, gain, bias, planes, conv_in, emb_in, time_in, up_in, down_in, cot_in,
    out_conv, out_up, out_down, s,
):
    n_chip = n_sp // 2
    width = emb_in.shape[1]
    hidden = up_in.shape[1]
    block = width // n_dp
    chans = conv_in.shape[1]
    rows, cols, in_chans = planes.shape[2:]
    pixels = rows * cols
    half = pixels // 2
    taps = conv_in.shape[0] // n_sp
    me = lax.axis_index("sp")
    image = lax.axis_index("dp")
    core = lax.rem(me, 2)
    chip = me // 2
    far = lax.rem(chip, 2)
    col = chip // 2
    n_col = n_chip // 2
    east_col, west_col = lax.rem(col + 1, n_col), lax.rem(col + n_col - 1, n_col)
    over_col = lax.rem(col + 2, n_col)
    sibling = chip * 2 + 1 - core
    chip_of = lambda at, level: at * 2 + level
    dev_of = lambda which: which * 2 + core
    z_chip = chip_of(col, 1 - far)
    east, west = dev_of(chip_of(east_col, far)), dev_of(chip_of(west_col, far))
    z_peer = dev_of(z_chip)

    def send(src, dst, sems, at_send, at_recv, **where):
        return pltpu.make_async_remote_copy(
            src_ref=src, dst_ref=dst, send_sem=sems.at[0, at_send], recv_sem=sems.at[1, at_recv],
            device_id=where, device_id_type=MESH,
        )

    def others(count, first, act):
        @pl.loop(1, count)
        def _(step):
            act(lax.rem(first + step, count))

    def every(count, act):
        @pl.loop(0, count)
        def _(step):
            act(step)

    barrier = pltpu.get_barrier_semaphore()
    others(n_sp, me, lambda p: pl.semaphore_signal(barrier, 1, device_id={"sp": p}, device_id_type=MESH))
    others(n_dp, image, lambda p: pl.semaphore_signal(barrier, 1, device_id={"dp": p}, device_id_type=MESH))

    loads = {}
    for index, (name, src, dst) in enumerate(
        (
            ("conv", conv_in, s.conv),
            ("emb", emb_in, s.emb),
            ("up", up_in, s.up),
        )
    ):
        loads[name] = pltpu.make_async_copy(src, dst, s.load.at[index])

    def cot_load(p):
        columns = pl.ds(pl.multiple_of(p * block, block), block)
        return pltpu.make_async_copy(cot_in.at[:, columns], s.cot.at[p, chip], s.load.at[8 + p])

    my_rows = pl.ds(pl.multiple_of(core * hidden, hidden), hidden)
    its_rows = pl.ds(pl.multiple_of((1 - core) * hidden, hidden), hidden)

    def down_load(p):
        columns = pl.ds(pl.multiple_of(p * block, block), block)
        return pltpu.make_async_copy(
            down_in.at[:, columns], s.gated.at[p, my_rows], s.load.at[8 + n_dp + p]
        )

    def time_load(k):
        columns = pl.ds(pl.multiple_of(k * 1024, 1024), 1024)
        return pltpu.make_async_copy(time_in.at[:, columns], s.time.at[k], s.load.at[8 + 2 * n_dp + k])

    n_time = 3 * width // 1024

    loads["conv"].start()
    every(n_dp, lambda p: cot_load(p).start())
    every(n_dp, lambda p: down_load(p).start())
    every(n_time, lambda k: time_load(k).start())
    for name in ("emb", "up"):
        loads[name].start()

    n_row = n_dp // 2
    row_at = lax.rem(image, n_row)
    row_first = image - row_at
    twin = lax.rem(image + n_row, n_dp)

    def in_row(act):
        others(n_row, row_at, lambda at: act(row_first + at))

    def aim(q):
        step = lax.rem(q, n_row - 1)
        away = (1 - q // (n_dp - 2)) * (1 + 2 * step - 3 * (step // 2))
        swap = lax.rem(q // (n_row - 1) + 1, 2) - q // (n_dp - 1)
        return swap, lax.rem(row_at + away, n_row)

    def turn(q):
        swap, at = aim(q)
        return lax.rem(row_first + swap * n_row, n_dp) + at

    top, low = pl.ds(0, half), pl.ds(half, half)
    n_late = pixels * 3 // 8
    late, early = pl.ds(0, n_late), pl.ds(n_late, pixels - n_late)
    early_top, early_low = pl.ds(n_late, n_late), pl.ds(2 * n_late, pixels - 2 * n_late)
    routes = {
        "z": (chip, None, z_peer, z_chip),
        "e": (chip, None, east, chip_of(west_col, far)),
        "w": (chip, None, west, chip_of(east_col, far)),
        "ez": (z_chip, early, east, chip_of(west_col, 1 - far)),
        "wz": (z_chip, early, west, chip_of(east_col, 1 - far)),
        "ee": (chip_of(west_col, far), top, east, chip_of(over_col, far)),
        "ww": (chip_of(east_col, far), low, west, chip_of(over_col, far)),
        "eez": (chip_of(west_col, 1 - far), early_top, east, chip_of(over_col, 1 - far)),
        "wwz": (chip_of(east_col, 1 - far), early_low, west, chip_of(over_col, 1 - far)),
        "ze": (chip_of(west_col, far), late, z_peer, chip_of(west_col, 1 - far)),
        "zw": (chip_of(east_col, far), late, z_peer, chip_of(east_col, 1 - far)),
        "zo": (chip_of(over_col, far), late, z_peer, chip_of(over_col, 1 - far)),
    }
    order = {name: index for index, name in enumerate(routes)}

    def cot_copy(name, p, arriving=False):
        mine, part, to, theirs = routes[name]
        which = theirs if arriving else mine
        ref = s.cot.at[p, which] if part is None else s.cot.at[p, which, part, :]
        at = order[name] * n_dp + p
        return send(ref, ref, s.cot_sem, at, at, sp=to)

    def across(q):
        cot_copy("z", turn(q)).start()

    def beside(q):
        p = turn(q)
        cot_copy("e", p).start()
        cot_copy("w", p).start()

    def relay(q, steps):
        p = turn(q)
        for name, then in steps:
            cot_copy(name, p, True).wait_recv()
            for onward in then:
                cot_copy(onward, p).start()

    def relay_near(q):
        relay(q, (("z", ("ez", "wz")), ("e", ("ee", "ze")), ("w", ("ww", "zw"))))

    def relay_far(q):
        relay(q, (("ez", ("eez",)), ("wz", ("wwz",)), ("ee", ("zo",))))

    def landed(q):
        p = turn(q)
        for name in ("ww", "eez", "wwz", "ze", "zw", "zo"):
            cot_copy(name, p, True).wait_recv()

    for parity in range(2):
        s.rim_tx[parity] = planes[parity, 1].astype(F32)[:, cols - 1, :].astype(BF16)

    @pl.when(me == 0)
    def _():
        s.rim_rx[...] = jnp.zeros_like(s.rim_rx)

    pl.semaphore_wait(barrier, n_sp - 1 + n_dp - 1)
    rim_copy = send(s.rim_tx, s.rim_rx, s.pair_sem, 5, 5, sp=lax.rem(me + 1, n_sp))

    @pl.when(me < n_sp - 1)
    def _():
        rim_copy.start()

    every(n_dp, lambda p: cot_load(p).wait())
    for q in range(2):
        across(q)
        beside(q)

    first_column = lax.broadcasted_iota(jnp.int32, (rows, cols, in_chans), 1) == 0

    def patch(row_tap, col_tap):
        parity = (row_tap + 1) % 2
        value = planes[parity, (col_tap + 1) % 2].astype(F32)
        if col_tap == 0:
            value = pltpu.roll(value, 1, 1)
            value = jnp.where(first_column, s.rim_rx[parity].astype(F32)[:, None, :], value)
        if row_tap == 0:
            value = jnp.concatenate([jnp.zeros_like(value[:1]), value[:-1]], axis=0)
        tap = row_tap * 3 + col_tap
        s.patches[:, tap * in_chans : (tap + 1) * in_chans] = value.reshape(pixels, in_chans).astype(BF16)

    for row_tap in range(3):
        for col_tap in (1, 2):
            patch(row_tap, col_tap)
    loads["conv"].wait()

    @pl.when(me > 0)
    def _():
        rim_copy.wait_recv()

    for row_tap in range(3):
        patch(row_tap, 0)
    s.z[...] = nn(s.patches[...], s.conv[...])
    z = s.z[...]
    s.stat_tx[...] = rows_of(
        jnp.sum(z, axis=0, keepdims=True), jnp.sum(z * z, axis=0, keepdims=True), (8, chans)
    )
    s.stat_rx[me] = s.stat_tx[...]

    def stat_copy(p):
        return send(s.stat_tx, s.stat_rx.at[me], s.stat_sem, p, me, sp=p)

    def stat_from(p):
        return send(s.stat_tx, s.stat_rx.at[p], s.stat_sem, p, p, sp=p)

    others(n_sp, me, lambda p: stat_copy(p).start())
    across(2)
    across(3)
    relay_near(0)
    beside(2)

    every(n_dp, lambda p: down_load(p).wait())
    my_down, its_down = s.gated.at[:, my_rows], s.gated.at[:, its_rows]
    down_copy = send(my_down, my_down, s.pair_sem, 0, 0, sp=sibling)
    down_copy.start()

    def mod_part(k):
        columns = pl.ds(pl.multiple_of(k * 1024, 1024), 1024)
        time_load(k).wait()
        s.mod[:, columns] = nn(es[...], s.time[k])

    every(n_time, mod_part)

    others(n_sp, me, lambda p: stat_from(p).wait_recv())
    count = pixels * n_sp * (chans // NORM_GROUPS)
    shift_by = (chans // NORM_GROUPS).bit_length() - 1

    def group_sums(ref):
        pair = lax.broadcasted_iota(jnp.int32, (chans, chans), 0) >> shift_by
        other = lax.broadcasted_iota(jnp.int32, (chans, chans), 1) >> shift_by
        same = jnp.where(pair == other, 1.0, 0.0).astype(F32)
        totals = exact(jnp.sum(ref[...], axis=0), same, ((1,), (0,))) / count
        return totals[0:1, :], totals[1:2, :]

    mean, square = group_sums(s.stat_rx)
    rstd = lax.rsqrt(square - mean * mean + 1e-05)
    s.rstd[...] = jnp.broadcast_to(rstd, s.rstd.shape)
    xhat = (s.z[...] - mean) * rstd
    s.z[...] = xhat
    pre = xhat * gain[...] + bias[...]
    sigma = jax.nn.sigmoid(pre)
    s.slope0[...] = sigma * (1.0 + pre * (1.0 - sigma)) * gain[...]
    act = (pre * sigma).reshape(n_chip, 2, pixels // n_sp, chans)
    for k in range(2):
        s.act_tx[k] = act[:, k].reshape(half, chans).astype(BF16)
    s.act_rx[me] = s.act_tx[core]

    def act_copy(p, source):
        return send(s.act_tx.at[lax.rem(p, 2)], s.act_rx.at[source], s.act_sem, p, source, sp=p)

    others(n_sp, me, lambda p: act_copy(p, me).start())
    for q in range(4, n_dp):
        across(q)
    relay_near(1)
    beside(3)
    relay_far(0)

    loads["emb"].wait()
    loads["up"].wait()
    ones = jnp.ones((16, width), BF16)
    mean_row = nt(ones, s.emb[...])[0:1, :] / width
    s.mean_col[...] = jnp.broadcast_to(
        jnp.mean(s.emb[...].astype(F32), axis=1, keepdims=True), s.mean_col.shape
    )
    mean_col = s.mean_col[:, 0:1]
    s.gram[...] = jnp.zeros_like(s.gram)
    s.mix[...] = jnp.zeros_like(s.mix)
    s.offset[...] = jnp.zeros_like(s.offset)
    s.skip[...] = jnp.zeros_like(s.skip)

    def fold(p):
        columns = pl.ds(pl.multiple_of(p * block, block), block)
        emb = s.emb[:, columns]
        scale = s.mod[0:1, pl.ds(pl.multiple_of(width + p * block, block), block)]
        left = ((emb.astype(F32) - mean_col) * (1.0 + scale)).astype(BF16)
        up = s.up[columns, :]
        s.mix[...] += nn(left, up)
        s.gram[...] += nt(emb, emb)
        high, low_part = split(s.mod[:, columns])
        s.offset[...] += nn(high, up) + nn(low_part, up)
        s.skip[...] += nt(s.cot[p, chip], emb)

    every(n_dp, fold)
    my_cols, its_cols = my_rows, its_rows
    s.mixer[:, my_cols] = s.mix[...].astype(BF16)
    s.offsets[:, my_cols] = s.offset[...]
    mix_copy = send(s.mixer.at[:, my_cols], s.mixer.at[:, my_cols], s.pair_sem, 1, 1, sp=sibling)
    mix_copy.start()
    off_copy = send(s.offsets.at[:, my_cols], s.offsets.at[:, my_cols], s.pair_sem, 2, 2, sp=sibling)
    off_copy.start()
    relay_near(2)
    beside(4)
    relay_far(1)

    down_from = send(its_down, its_down, s.pair_sem, 0, 0, sp=sibling)
    down_copy.wait_send()
    down_from.wait_recv()

    def gate_part(p):
        gate = s.mod[0:1, pl.ds(pl.multiple_of(2 * width + p * block, block), block)]
        s.gated[p] = (s.gated[p].astype(F32) * gate).astype(BF16)

    every(n_dp, gate_part)

    others(n_sp, me, lambda p: act_copy(p, p).wait_recv())

    def place(p):
        tile = s.act_rx[p].astype(F32).reshape(n_chip, pixels // n_sp, chans)
        s.act[:, pl.ds(pl.multiple_of(p * 8, 8), 8), :] = tile

    every(n_sp, place)
    mix_from = send(s.mixer.at[:, its_cols], s.mixer.at[:, its_cols], s.pair_sem, 1, 1, sp=sibling)
    off_from = send(s.offsets.at[:, its_cols], s.offsets.at[:, its_cols], s.pair_sem, 2, 2, sp=sibling)
    mix_from.wait_recv()
    off_from.wait_recv()
    gram_hi, gram_lo = split(s.gram[...] - width * mean_col * mean_row)
    s.gram_hi[...] = gram_hi
    s.gram_lo[...] = gram_lo

    def forward(i):
        lanes = pl.ds(pl.multiple_of(i * pixels, pixels), pixels)
        wide = s.act[i]
        narrow = wide.astype(BF16)
        spread = nn(narrow, s.gram_hi[...]) + nn(narrow, s.gram_lo[...])
        var = jnp.sum(wide * spread, axis=-1, keepdims=True) / width
        token_rstd = lax.rsqrt(var + 1e-06)
        moved = nn(narrow, s.mixer[...]) * token_rstd
        value, slope = gelu_pair(moved + s.offsets[0:1, :])
        s.hid_t[:, lanes] = value.T.astype(BF16)
        s.act_t[:, lanes] = wide.T.astype(BF16)
        s.slope[i] = slope
        s.moved[i] = moved
        s.spread[i] = spread * (token_rstd / width)
        s.token_rstd[i] = jnp.broadcast_to(token_rstd, (pixels, 128))
        s.dhid[i] = jnp.zeros_like(slope)

    relay_near(3)
    beside(5)
    relay_far(2)
    every(n_chip, forward)
    s.patches_t[...] = s.patches[...].astype(F32).T.astype(BF16)

    def sib_copy(p):
        return send(s.sib_tx.at[p], s.sib_rx.at[p], s.sib_sem, p, p, sp=sibling)

    def down_out(q):
        swap, at = aim(q)
        p, slot = turn(q), swap * n_row + row_at
        return send(s.gd_tx.at[p], s.gd_rx.at[slot], s.gd_sem, p, slot, dp=row_first + at)

    def down_from(swap, act):
        def one(p):
            slot = swap * n_row + lax.rem(p, n_row)
            send(s.gd_tx.at[p], s.gd_rx.at[slot], s.gd_sem, p, slot, dp=p).wait_recv()
            act(s.gd_rx[slot].astype(F32))

        in_row(one)

    twin_out = send(s.gd_tx.at[twin], s.gd_twin, s.gd_sem, n_dp, n_dp, dp=twin)

    def block_of(q):
        p = turn(q)
        gate = s.mod[0:1, pl.ds(pl.multiple_of(2 * width + p * block, block), block)]
        cot = s.cot[p].reshape(n_chip * pixels, block)
        s.sib_tx[p] = (nn(s.hid_t[its_rows, :], cot) * gate).astype(BF16)
        sib_copy(p).start()
        s.gd_own[lax.rem(q, 2)] = nn(s.hid_t[my_rows, :], cot) * gate

        def part(h):
            rows = pl.ds(h * (n_chip // 2), n_chip // 2)
            tokens = s.cot[p, rows].reshape(n_chip // 2 * pixels, block)
            s.dhid[rows] += nt(tokens, s.gated[p]).reshape(n_chip // 2, pixels, 2 * hidden)

        every(2, part)

    def whole(q):
        p = turn(q)
        sib_copy(p).wait_recv()
        return p, s.gd_own[lax.rem(q, 2)] + s.sib_rx[p].astype(F32)

    def hand_over(q):
        p, total = whole(q)

        @pl.when(q < n_dp - 2)
        def _():
            s.gd_tx[p] = total.astype(BF16)
            down_out(q).start()

        @pl.when(q == n_dp - 2)
        def _():
            out_down[...] = total

            def add(value):
                out_down[...] += value

            down_from(1, add)
            s.gd_tx[twin] = out_down[...].astype(BF16)
            twin_out.start()

    @pl.loop(0, n_dp)
    def _(q):
        @pl.when(q + 6 < n_dp)
        def _():
            beside(q + 6)

        @pl.when(q + 4 < n_dp)
        def _():
            relay_near(q + 4)

        @pl.when(q + 3 < n_dp)
        def _():
            relay_far(q + 3)

        @pl.when(q > 0)
        def _():
            hand_over(q - 1)

        landed(q)
        block_of(q)

    s.du_sum[...] = jnp.zeros_like(s.du_sum)

    def backward(i):
        grad = s.dhid[i] * s.slope[i]
        s.du_sum[0:1, :] += jnp.sum(grad, axis=0, keepdims=True)
        grad = grad * s.token_rstd[i][:, 0:1]
        cross = jnp.sum(grad * s.moved[i], axis=-1, keepdims=True)
        narrow = grad.astype(BF16)
        s.du[pl.ds(pl.multiple_of(i * pixels, pixels), pixels), :] = narrow
        s.act[i] = nt(narrow, s.mixer[...]) - cross * s.spread[i]

    every(n_chip, backward)
    s.act[chip] += s.skip[...]

    def tile_of(p):
        rows = s.act[:, pl.ds(pl.multiple_of(p * 8, 8), 8), :]
        return rows.reshape(half, chans).astype(BF16)

    def part_copy(p, source):
        return send(s.part_tx.at[p], s.part_rx.at[source], s.part_sem, p, source, sp=p)

    def part_out(p):
        s.part_tx[p] = tile_of(p)
        part_copy(p, me).start()

    others(n_sp, me, part_out)
    s.part_rx[me] = tile_of(me)

    s.pairs[...] = nn(s.act_t[...], s.du[...])
    s.pair_tx[...] = s.pairs[:, its_cols].astype(BF16)
    s.sum_tx[...] = s.du_sum[:, its_cols]
    pair_copy = send(s.pair_tx, s.pair_rx, s.pair_sem, 3, 3, sp=sibling)
    pair_copy.start()
    sum_copy = send(s.sum_tx, s.sum_rx, s.pair_sem, 4, 4, sp=sibling)
    sum_copy.start()
    _, total = whole(n_dp - 1)
    out_down[...] = total

    pair_copy.wait_recv()
    sum_copy.wait_recv()
    s.q_tx[...] = (s.pairs[:, my_cols] + s.pair_rx[...].astype(F32)).astype(BF16)
    s.q_rx[image] = s.q_tx[...]
    du_sum = (s.du_sum[:, my_cols] + s.sum_rx[...])[0:1, :]

    def side_of(p):
        shift = s.mod[0:1, pl.ds(pl.multiple_of(p * block, block), block)]
        scale = s.mod[0:1, pl.ds(pl.multiple_of(width + p * block, block), block)]
        which = lax.broadcasted_iota(jnp.int32, (8, block), 0)
        return jnp.where(which == 2, du_sum, rows_of(1.0 + scale, shift, (8, block)))

    def q_copy(p, source):
        return send(s.q_tx, s.q_rx.at[source], s.q_sem, p, source, dp=p)

    def side_copy(p, source):
        return send(s.side_tx.at[p], s.side_rx.at[source], s.side_sem, p, source, dp=p)

    def forward_copy(p):
        at = lax.rem(p + n_row, n_dp)
        return send(s.q_rx.at[twin], s.q_rx.at[twin], s.q_sem, at, twin, dp=p)

    def side_out(p):
        s.side_tx[p] = side_of(p)
        side_copy(p, image).start()

    q_copy(twin, image).start()
    in_row(lambda p: q_copy(p, image).start())
    others(n_dp, image, side_out)
    s.side_rx[image] = side_of(image)

    others(n_sp, me, lambda p: part_copy(p, p).wait_recv())
    parts = []
    for k in range(2):
        total = s.part_rx[k].astype(F32)
        for j in range(1, n_chip):
            total = total + s.part_rx[2 * j + k].astype(F32)
        parts.append(total.reshape(n_chip, 1, pixels // n_sp, chans))
    dx = jnp.concatenate(parts, axis=1).reshape(pixels, chans) * s.slope0[...]
    s.slope0[...] = dx
    s.stat2_tx[...] = rows_of(
        jnp.sum(dx, axis=0, keepdims=True), jnp.sum(dx * s.z[...], axis=0, keepdims=True), (8, chans)
    )
    s.stat2_rx[me] = s.stat2_tx[...]

    def stat2_copy(p, source):
        return send(s.stat2_tx, s.stat2_rx.at[source], s.stat2_sem, p, source, sp=p)

    others(n_sp, me, lambda p: stat2_copy(p, me).start())

    others(n_sp, me, lambda p: stat2_copy(p, p).wait_recv())
    first, second = group_sums(s.stat2_rx)
    dz = (s.rstd[0:1, :] * (s.slope0[...] - first - s.z[...] * second)).astype(BF16)
    s.grad[...] = nn(s.patches_t[...], dz)

    def rows_at(k):
        return pl.ds(pl.multiple_of(k * taps, 8), taps)

    n_half = 2
    lanes_of = lambda h: slice(h * (chans // n_half), (h + 1) * (chans // n_half))

    def grad_copy(h, p, source):
        at = h * n_sp
        return send(s.grad_tx.at[h, p], s.grad_rx.at[h, source], s.grad_sem, at + p, at + source, sp=p)

    def all_copy(h, p, source):
        at = h * n_dp
        return send(s.all_tx.at[h], s.all_rx.at[h, source], s.all_sem, at + p, at + source, dp=p)

    def last_copy(h, p, source):
        at = h * n_sp
        return send(s.last_tx.at[h], s.last_rx.at[h, source], s.last_sem, at + p, at + source, sp=p)

    for h in range(n_half):

        def grad_out(p, h=h):
            s.grad_tx[h, p] = s.grad[rows_at(p), lanes_of(h)].astype(BF16)
            grad_copy(h, p, me).start()

        others(n_sp, me, grad_out)
        s.grad_rx[h, me] = s.grad[rows_at(me), lanes_of(h)].astype(BF16)

    def slots(ref, h, n):
        total = ref[h, 0].astype(F32)
        for j in range(1, n):
            total = total + ref[h, j].astype(F32)
        return total

    for h in range(n_half):
        others(n_sp, me, lambda p: grad_copy(h, p, p).wait_recv())
        s.all_tx[h] = slots(s.grad_rx, h, n_sp).astype(BF16)
        s.all_rx[h, image] = s.all_tx[h]
        others(n_dp, image, lambda p: all_copy(h, p, image).start())

    q_copy(twin, twin).wait_recv()
    in_row(lambda p: forward_copy(p).start())

    for h in range(n_half):
        others(n_dp, image, lambda p: all_copy(h, p, p).wait_recv())
        s.last_tx[h] = slots(s.all_rx, h, n_dp).astype(BF16)
        s.last_rx[h, me] = s.last_tx[h]
        others(n_sp, me, lambda p: last_copy(h, p, me).start())

    def add_down(value):
        out_down[...] += value

    down_from(0, add_down)
    twin_out.wait_recv()
    add_down(s.gd_twin[...].astype(F32))

    in_row(lambda p: q_copy(p, p).wait_recv())
    in_row(lambda p: q_copy(p, lax.rem(p + n_row, n_dp)).wait_recv())
    others(n_dp, image, lambda p: side_copy(p, p).wait_recv())
    here = s.emb[:, pl.ds(pl.multiple_of(image * block, block), block)].astype(F32) - mean_col
    here_t = here.T
    s.emb_t[...] = here_t
    which = lax.broadcasted_iota(jnp.int32, (n_dp, block), 0)
    shifts = jnp.zeros((n_dp, block), F32)
    sums = jnp.zeros((n_dp, block), F32)
    for k in range(n_dp):
        shifts = jnp.where(which == k, s.side_rx[k, 1:2, :], shifts)
        sums = jnp.where(which == k, s.side_rx[k, 2:3, :], sums)
    out_up[...] = exact(shifts, sums, ((0,), (0,)))

    def up_part(k):
        left = here_t * s.side_rx[k].T[:, 0:1]
        out_up[...] += nn(left.astype(BF16), s.q_rx[k])

    for k in range(n_dp):
        up_part(k)

    for h in range(n_half):
        others(n_sp, me, lambda p: last_copy(h, p, p).wait_recv())

        def show(k, h=h):
            out_conv[rows_at(k), lanes_of(h)] = s.last_rx[h, k].astype(F32)

        every(n_sp, show)

    for copy in (mix_copy, off_copy, pair_copy, sum_copy):
        copy.wait_send()

    @pl.when(me < n_sp - 1)
    def _():
        rim_copy.wait_send()

    def left(p):
        for copy in (stat_copy(p), act_copy(p, me), part_copy(p, me), stat2_copy(p, me)):
            copy.wait_send()
        for h in range(n_half):
            grad_copy(h, p, me).wait_send()
            last_copy(h, p, me).wait_send()

    others(n_sp, me, left)

    def left_dp(p):
        for copy in (q_copy(p, image), side_copy(p, image)):
            copy.wait_send()
        for h in range(n_half):
            all_copy(h, p, image).wait_send()

    others(n_dp, image, left_dp)

    every(n_dp - 2, lambda q: down_out(q).wait_send())
    twin_out.wait_send()

    def left_block(p):
        sib_copy(p).wait_send()
        for name in routes:
            cot_copy(name, p).wait_send()

    every(n_dp, left_block)


class Scratch:
    def __init__(self, names, refs):
        for name, ref in zip(names, refs):
            setattr(self, name, ref)


def on_device(
    n_sp, n_dp, feats, conv_w, group_norm_gain, group_norm_bias, emb_w, time_w, up_w, down_w, steps, cotangent
):
    image = feats[0]
    rows_in, cols_in, in_chans = image.shape
    rows, cols = rows_in // 2, cols_in // 2
    pixels = rows * cols
    planes = image.reshape(rows, 2, cols, 2, in_chans).transpose(1, 3, 0, 2, 4)
    freq_count = time_w.shape[0] // 2
    freqs = jnp.exp(-math.log(10000.0) * jnp.arange(freq_count, dtype=F32) / freq_count)
    angle = steps[0].astype(F32) * freqs
    embed = jax.nn.silu(jnp.concatenate([jnp.cos(angle), jnp.sin(angle)])).astype(BF16)
    es = jnp.broadcast_to(embed[None, :], (16, embed.shape[0]))
    chans = conv_w.shape[1]
    width = emb_w.shape[1]
    hidden = up_w.shape[1]
    block = width // n_dp
    n_chip = n_sp // 2
    taps = conv_w.shape[0] // n_sp
    half = pixels // 2
    tokens = n_chip * pixels
    vm = pltpu.VMEM
    dma = lambda n: pltpu.SemaphoreType.DMA((2, n))
    scratch = dict(
        load=pltpu.SemaphoreType.DMA((8 + 2 * n_dp + time_w.shape[1] // 1024,)),
        stat_sem=dma(n_sp), act_sem=dma(n_sp), part_sem=dma(n_sp), stat2_sem=dma(n_sp),
        grad_sem=dma(2 * n_sp), last_sem=dma(2 * n_sp), cot_sem=dma(12 * n_dp), pair_sem=dma(8),
        sib_sem=dma(n_dp), gd_sem=dma(n_dp + 1), q_sem=dma(n_dp), side_sem=dma(n_dp), all_sem=dma(2 * n_dp),
        patches=vm((pixels, 9 * in_chans), BF16), rim_tx=vm((2, rows, in_chans), BF16),
        rim_rx=vm((2, rows, in_chans), BF16), conv=vm(conv_w.shape, BF16), emb=vm(emb_w.shape, BF16),
        time=vm((time_w.shape[1] // 1024, time_w.shape[0], 1024), BF16), up=vm(up_w.shape, BF16),
        gated=vm((n_dp, 2 * hidden, block), BF16), cot=vm((n_dp, n_chip, pixels, block), BF16),
        z=vm((pixels, chans), F32), slope0=vm((pixels, chans), F32), rstd=vm((8, chans), F32),
        stat_tx=vm((8, chans), F32), stat_rx=vm((n_sp, 8, chans), F32),
        stat2_tx=vm((8, chans), F32), stat2_rx=vm((n_sp, 8, chans), F32),
        mod=vm((16, 3 * width), F32), act_tx=vm((2, half, chans), BF16),
        act_rx=vm((n_sp, half, chans), BF16), act=vm((n_chip, pixels, chans), F32),
        act_t=vm((chans, tokens), BF16), mean_col=vm((chans, 128), F32), gram=vm((chans, chans), F32),
        gram_hi=vm((chans, chans), BF16), gram_lo=vm((chans, chans), BF16),
        mix=vm((chans, hidden), F32), mixer=vm((chans, 2 * hidden), BF16),
        offset=vm((16, hidden), F32), offsets=vm((16, 2 * hidden), F32), skip=vm((pixels, chans), F32),
        hid_t=vm((2 * hidden, tokens), BF16), slope=vm((n_chip, pixels, 2 * hidden), F32),
        moved=vm((n_chip, pixels, 2 * hidden), F32), dhid=vm((n_chip, pixels, 2 * hidden), F32),
        spread=vm((n_chip, pixels, chans), F32), token_rstd=vm((n_chip, pixels, 128), F32),
        patches_t=vm((9 * in_chans, pixels), BF16),
        sib_tx=vm((n_dp, hidden, block), BF16), sib_rx=vm((n_dp, hidden, block), BF16),
        gd_own=vm((2, hidden, block), F32), gd_tx=vm((n_dp, hidden, block), BF16),
        gd_rx=vm((n_dp, hidden, block), BF16), gd_twin=vm((hidden, block), BF16), du_sum=vm((8, 2 * hidden), F32),
        du=vm((tokens, 2 * hidden), BF16), part_tx=vm((n_sp, half, chans), BF16),
        part_rx=vm((n_sp, half, chans), BF16), pairs=vm((chans, 2 * hidden), F32),
        pair_tx=vm((chans, hidden), BF16), pair_rx=vm((chans, hidden), BF16),
        sum_tx=vm((8, hidden), F32), sum_rx=vm((8, hidden), F32), q_tx=vm((chans, hidden), BF16),
        q_rx=vm((n_dp, chans, hidden), BF16), side_tx=vm((n_dp, 8, block), F32),
        side_rx=vm((n_dp, 8, block), F32), grad=vm((conv_w.shape[0], chans), F32),
        grad_tx=vm((2, n_sp, taps, chans // 2), BF16), grad_rx=vm((2, n_sp, taps, chans // 2), BF16),
        all_tx=vm((2, taps, chans // 2), BF16), all_rx=vm((2, n_dp, taps, chans // 2), BF16),
        last_tx=vm((2, taps, chans // 2), BF16), last_rx=vm((2, n_sp, taps, chans // 2), BF16),
        emb_t=vm((block, chans), F32),
    )
    names = tuple(scratch)

    def kernel(*refs):
        body(n_sp, n_dp, *refs[:13], Scratch(names, refs[13:]))

    in_vmem = pl.BlockSpec(memory_space=pltpu.VMEM)
    in_place = pl.BlockSpec(memory_space=pl.ANY)
    return pl.pallas_call(
        kernel,
        out_shape=(
            jax.ShapeDtypeStruct(conv_w.shape, F32),
            jax.ShapeDtypeStruct((block, hidden), F32),
            jax.ShapeDtypeStruct((hidden, block), F32),
        ),
        in_specs=[in_vmem] * 4 + [in_place] * 6,
        out_specs=(in_vmem,) * 3,
        scratch_shapes=list(scratch.values()),
        compiler_params=pltpu.CompilerParams(
            collective_id=0, has_side_effects=True, vmem_limit_bytes=67043328
        ),
    )(es, group_norm_gain[None], group_norm_bias[None], planes, conv_w, emb_w, time_w, up_w, down_w, cotangent[0])


def solution(mesh):
    in_specs = (
        P("dp", None, "sp", None),
        P(),
        P(),
        P(),
        P(),
        P(),
        P(None, "sp"),
        P("sp", None),
        P("dp"),
        P("dp", "sp", None),
    )
    out_specs = (P(), P("dp", "sp"), P("sp", "dp"))
    return jax.shard_map(
        functools.partial(on_device, mesh.shape["sp"], mesh.shape["dp"]),
        mesh=mesh,
        in_specs=in_specs,
        out_specs=out_specs,
        check_vma=False,
    )
```

```python
import functools
import math

import jax
import jax.numpy as jnp
from jax import lax
from jax.experimental import pallas as pl
from jax.experimental.pallas import tpu as pltpu
from jax.sharding import PartitionSpec as P

NORM_GROUPS = 32
F32 = jnp.float32
BF16 = jnp.bfloat16
MESH = pl.DeviceIdType.MESH


def gelu_pair(u):
    coef = math.sqrt(2.0 / math.pi)
    inner = coef * (u + 0.044715 * u * u * u)
    tangent = jnp.tanh(inner)
    value = 0.5 * u * (1.0 + tangent)
    slope = 0.5 * (1.0 + tangent) + 0.5 * u * (1.0 - tangent * tangent) * coef * (
        1.0 + 3.0 * 0.044715 * u * u
    )
    return (value, slope)


def nn(left, right):
    return lax.dot_general(left, right, (((1,), (0,)), ((), ())), preferred_element_type=F32)


def nt(left, right):
    return lax.dot_general(left, right, (((1,), (1,)), ((), ())), preferred_element_type=F32)


def exact(left, right, dims):
    return lax.dot_general(
        left,
        right,
        (dims, ((), ())),
        precision=lax.Precision.HIGHEST,
        preferred_element_type=F32,
    )


def split(value):
    high = value.astype(BF16)
    return high, (value - high.astype(F32)).astype(BF16)


def rows_of(first, second, like):
    which = lax.broadcasted_iota(jnp.int32, like, 0)
    return jnp.where(which == 0, first, jnp.where(which == 1, second, 0.0))


def body(
    n_sp, n_dp, es, gain, bias, planes, conv_in, emb_in, time_in, up_in, down_in, cot_in,
    out_conv, out_up, out_down, s,
):
    n_chip = n_sp // 2
    width = emb_in.shape[1]
    hidden = up_in.shape[1]
    block = width // n_dp
    chans = conv_in.shape[1]
    rows, cols, in_chans = planes.shape[2:]
    pixels = rows * cols
    half = pixels // 2
    taps = conv_in.shape[0] // n_sp
    me = lax.axis_index("sp")
    image = lax.axis_index("dp")
    core = lax.rem(me, 2)
    chip = me // 2
    far = lax.rem(chip, 2)
    col = chip // 2
    n_col = n_chip // 2
    east_col, west_col = lax.rem(col + 1, n_col), lax.rem(col + n_col - 1, n_col)
    over_col = lax.rem(col + 2, n_col)
    sibling = chip * 2 + 1 - core
    chip_of = lambda at, level: at * 2 + level
    dev_of = lambda which: which * 2 + core
    z_chip = chip_of(col, 1 - far)
    east, west = dev_of(chip_of(east_col, far)), dev_of(chip_of(west_col, far))
    z_peer = dev_of(z_chip)

    def send(src, dst, sems, at_send, at_recv, **where):
        return pltpu.make_async_remote_copy(
            src_ref=src, dst_ref=dst, send_sem=sems.at[0, at_send], recv_sem=sems.at[1, at_recv],
            device_id=where, device_id_type=MESH,
        )

    def others(count, first, act):
        @pl.loop(1, count)
        def _(step):
            act(lax.rem(first + step, count))

    def every(count, act):
        @pl.loop(0, count)
        def _(step):
            act(step)

    barrier = pltpu.get_barrier_semaphore()
    others(n_sp, me, lambda p: pl.semaphore_signal(barrier, 1, device_id={"sp": p}, device_id_type=MESH))
    others(n_dp, image, lambda p: pl.semaphore_signal(barrier, 1, device_id={"dp": p}, device_id_type=MESH))

    loads = {}
    for index, (name, src, dst) in enumerate(
        (
            ("conv", conv_in, s.conv),
            ("emb", emb_in, s.emb),
            ("up", up_in, s.up),
        )
    ):
        loads[name] = pltpu.make_async_copy(src, dst, s.load.at[index])

    def cot_load(p):
        columns = pl.ds(pl.multiple_of(p * block, block), block)
        return pltpu.make_async_copy(cot_in.at[:, columns], s.cot.at[p, chip], s.load.at[8 + p])

    my_rows = pl.ds(pl.multiple_of(core * hidden, hidden), hidden)
    its_rows = pl.ds(pl.multiple_of((1 - core) * hidden, hidden), hidden)

    def down_load(p):
        columns = pl.ds(pl.multiple_of(p * block, block), block)
        return pltpu.make_async_copy(
            down_in.at[:, columns], s.gated.at[p, my_rows], s.load.at[8 + n_dp + p]
        )

    def time_load(k):
        columns = pl.ds(pl.multiple_of(k * 1024, 1024), 1024)
        return pltpu.make_async_copy(time_in.at[:, columns], s.time.at[k], s.load.at[8 + 2 * n_dp + k])

    n_time = 3 * width // 1024

    loads["conv"].start()
    every(n_dp, lambda p: cot_load(p).start())
    every(n_dp, lambda p: down_load(p).start())
    every(n_time, lambda k: time_load(k).start())
    for name in ("emb", "up"):
        loads[name].start()

    n_row = n_dp // 2
    row_at = lax.rem(image, n_row)
    row_first = image - row_at
    twin = lax.rem(image + n_row, n_dp)

    def in_row(act):
        others(n_row, row_at, lambda at: act(row_first + at))

    def aim(q):
        step = lax.rem(q, n_row - 1)
        away = (1 - q // (n_dp - 2)) * (1 + 2 * step - 3 * (step // 2))
        swap = lax.rem(q // (n_row - 1) + 1, 2) - q // (n_dp - 1)
        return swap, lax.rem(row_at + away, n_row)

    def turn(q):
        swap, at = aim(q)
        return lax.rem(row_first + swap * n_row, n_dp) + at

    top, low = pl.ds(0, half), pl.ds(half, half)
    n_late = pixels * 3 // 8
    late, early = pl.ds(0, n_late), pl.ds(n_late, pixels - n_late)
    early_top, early_low = pl.ds(n_late, n_late), pl.ds(2 * n_late, pixels - 2 * n_late)
    routes = {
        "z": (chip, None, z_peer, z_chip),
        "e": (chip, None, east, chip_of(west_col, far)),
        "w": (chip, None, west, chip_of(east_col, far)),
        "ez": (z_chip, early, east, chip_of(west_col, 1 - far)),
        "wz": (z_chip, early, west, chip_of(east_col, 1 - far)),
        "ee": (chip_of(west_col, far), top, east, chip_of(over_col, far)),
        "ww": (chip_of(east_col, far), low, west, chip_of(over_col, far)),
        "eez": (chip_of(west_col, 1 - far), early_top, east, chip_of(over_col, 1 - far)),
        "wwz": (chip_of(east_col, 1 - far), early_low, west, chip_of(over_col, 1 - far)),
        "ze": (chip_of(west_col, far), late, z_peer, chip_of(west_col, 1 - far)),
        "zw": (chip_of(east_col, far), late, z_peer, chip_of(east_col, 1 - far)),
        "zo": (chip_of(over_col, far), late, z_peer, chip_of(over_col, 1 - far)),
    }
    order = {name: index for index, name in enumerate(routes)}

    def cot_copy(name, p, arriving=False):
        mine, part, to, theirs = routes[name]
        which = theirs if arriving else mine
        ref = s.cot.at[p, which] if part is None else s.cot.at[p, which, part, :]
        at = order[name] * n_dp + p
        return send(ref, ref, s.cot_sem, at, at, sp=to)

    def across(q):
        cot_copy("z", turn(q)).start()

    def beside(q):
        p = turn(q)
        cot_copy("e", p).start()
        cot_copy("w", p).start()

    def relay(q, steps):
        p = turn(q)
        for name, then in steps:
            cot_copy(name, p, True).wait_recv()
            for onward in then:
                cot_copy(onward, p).start()

    def relay_near(q):
        relay(q, (("z", ("ez", "wz")), ("e", ("ee", "ze")), ("w", ("ww", "zw"))))

    def relay_far(q):
        relay(q, (("ez", ("eez",)), ("wz", ("wwz",)), ("ee", ("zo",))))

    def landed(q):
        p = turn(q)
        for name in ("ww", "eez", "wwz", "ze", "zw", "zo"):
            cot_copy(name, p, True).wait_recv()

    for parity in range(2):
        s.rim_tx[parity] = planes[parity, 1].astype(F32)[:, cols - 1, :].astype(BF16)

    @pl.when(me == 0)
    def _():
        s.rim_rx[...] = jnp.zeros_like(s.rim_rx)

    pl.semaphore_wait(barrier, n_sp - 1 + n_dp - 1)
    rim_copy = send(s.rim_tx, s.rim_rx, s.pair_sem, 5, 5, sp=lax.rem(me + 1, n_sp))

    @pl.when(me < n_sp - 1)
    def _():
        rim_copy.start()

    every(n_dp, lambda p: cot_load(p).wait())
    across(0)
    across(1)
    beside(0)

    first_column = lax.broadcasted_iota(jnp.int32, (rows, cols, in_chans), 1) == 0

    def patch(row_tap, col_tap):
        parity = (row_tap + 1) % 2
        value = planes[parity, (col_tap + 1) % 2].astype(F32)
        if col_tap == 0:
            value = pltpu.roll(value, 1, 1)
            value = jnp.where(first_column, s.rim_rx[parity].astype(F32)[:, None, :], value)
        if row_tap == 0:
            value = jnp.concatenate([jnp.zeros_like(value[:1]), value[:-1]], axis=0)
        tap = row_tap * 3 + col_tap
        s.patches[:, tap * in_chans : (tap + 1) * in_chans] = value.reshape(pixels, in_chans).astype(BF16)

    for row_tap in range(3):
        for col_tap in (1, 2):
            patch(row_tap, col_tap)
    loads["conv"].wait()

    @pl.when(me > 0)
    def _():
        rim_copy.wait_recv()

    for row_tap in range(3):
        patch(row_tap, 0)
    s.z[...] = nn(s.patches[...], s.conv[...])
    z = s.z[...]
    s.stat_tx[...] = rows_of(
        jnp.sum(z, axis=0, keepdims=True), jnp.sum(z * z, axis=0, keepdims=True), (8, chans)
    )
    s.stat_rx[me] = s.stat_tx[...]

    def stat_copy(p):
        return send(s.stat_tx, s.stat_rx.at[me], s.stat_sem, p, me, sp=p)

    def stat_from(p):
        return send(s.stat_tx, s.stat_rx.at[p], s.stat_sem, p, p, sp=p)

    others(n_sp, me, lambda p: stat_copy(p).start())
    across(2)
    across(3)
    beside(1)
    relay_near(0)
    beside(2)

    every(n_dp, lambda p: down_load(p).wait())
    my_down, its_down = s.gated.at[:, my_rows], s.gated.at[:, its_rows]
    down_copy = send(my_down, my_down, s.pair_sem, 0, 0, sp=sibling)
    down_copy.start()

    def mod_part(k):
        columns = pl.ds(pl.multiple_of(k * 1024, 1024), 1024)
        time_load(k).wait()
        s.mod[:, columns] = nn(es[...], s.time[k])

    every(n_time, mod_part)

    others(n_sp, me, lambda p: stat_from(p).wait_recv())
    count = pixels * n_sp * (chans // NORM_GROUPS)
    shift_by = (chans // NORM_GROUPS).bit_length() - 1

    def group_sums(ref):
        pair = lax.broadcasted_iota(jnp.int32, (chans, chans), 0) >> shift_by
        other = lax.broadcasted_iota(jnp.int32, (chans, chans), 1) >> shift_by
        same = jnp.where(pair == other, 1.0, 0.0).astype(F32)
        totals = exact(jnp.sum(ref[...], axis=0), same, ((1,), (0,))) / count
        return totals[0:1, :], totals[1:2, :]

    mean, square = group_sums(s.stat_rx)
    rstd = lax.rsqrt(square - mean * mean + 1e-05)
    s.rstd[...] = jnp.broadcast_to(rstd, s.rstd.shape)
    xhat = (s.z[...] - mean) * rstd
    s.z[...] = xhat
    pre = xhat * gain[...] + bias[...]
    sigma = jax.nn.sigmoid(pre)
    s.slope0[...] = sigma * (1.0 + pre * (1.0 - sigma)) * gain[...]
    act = (pre * sigma).reshape(n_chip, 2, pixels // n_sp, chans)
    for k in range(2):
        s.act_tx[k] = act[:, k].reshape(half, chans).astype(BF16)
    s.act_rx[me] = s.act_tx[core]

    def act_copy(p, source):
        return send(s.act_tx.at[lax.rem(p, 2)], s.act_rx.at[source], s.act_sem, p, source, sp=p)

    others(n_sp, me, lambda p: act_copy(p, me).start())
    for q in range(4, n_dp):
        across(q)
    relay_near(1)
    beside(3)
    relay_far(0)

    loads["emb"].wait()
    loads["up"].wait()
    ones = jnp.ones((16, width), BF16)
    mean_row = nt(ones, s.emb[...])[0:1, :] / width
    s.mean_col[...] = jnp.broadcast_to(
        jnp.mean(s.emb[...].astype(F32), axis=1, keepdims=True), s.mean_col.shape
    )
    mean_col = s.mean_col[:, 0:1]
    s.gram[...] = jnp.zeros_like(s.gram)
    s.mix[...] = jnp.zeros_like(s.mix)
    s.offset[...] = jnp.zeros_like(s.offset)
    s.skip[...] = jnp.zeros_like(s.skip)

    def fold(p):
        columns = pl.ds(pl.multiple_of(p * block, block), block)
        emb = s.emb[:, columns]
        scale = s.mod[0:1, pl.ds(pl.multiple_of(width + p * block, block), block)]
        left = ((emb.astype(F32) - mean_col) * (1.0 + scale)).astype(BF16)
        up = s.up[columns, :]
        s.mix[...] += nn(left, up)
        s.gram[...] += nt(emb, emb)
        high, low_part = split(s.mod[:, columns])
        s.offset[...] += nn(high, up) + nn(low_part, up)
        s.skip[...] += nt(s.cot[p, chip], emb)

    every(n_dp, fold)
    my_cols, its_cols = my_rows, its_rows
    s.mixer[:, my_cols] = s.mix[...].astype(BF16)
    s.offsets[:, my_cols] = s.offset[...]
    mix_copy = send(s.mixer.at[:, my_cols], s.mixer.at[:, my_cols], s.pair_sem, 1, 1, sp=sibling)
    mix_copy.start()
    off_copy = send(s.offsets.at[:, my_cols], s.offsets.at[:, my_cols], s.pair_sem, 2, 2, sp=sibling)
    off_copy.start()
    relay_near(2)
    beside(4)
    relay_far(1)

    down_from = send(its_down, its_down, s.pair_sem, 0, 0, sp=sibling)
    down_copy.wait_send()
    down_from.wait_recv()

    def gate_part(p):
        gate = s.mod[0:1, pl.ds(pl.multiple_of(2 * width + p * block, block), block)]
        s.gated[p] = (s.gated[p].astype(F32) * gate).astype(BF16)

    every(n_dp, gate_part)

    others(n_sp, me, lambda p: act_copy(p, p).wait_recv())

    def place(p):
        tile = s.act_rx[p].astype(F32).reshape(n_chip, pixels // n_sp, chans)
        s.act[:, pl.ds(pl.multiple_of(p * 8, 8), 8), :] = tile

    every(n_sp, place)
    mix_from = send(s.mixer.at[:, its_cols], s.mixer.at[:, its_cols], s.pair_sem, 1, 1, sp=sibling)
    off_from = send(s.offsets.at[:, its_cols], s.offsets.at[:, its_cols], s.pair_sem, 2, 2, sp=sibling)
    mix_from.wait_recv()
    off_from.wait_recv()
    gram_hi, gram_lo = split(s.gram[...] - width * mean_col * mean_row)
    s.gram_hi[...] = gram_hi
    s.gram_lo[...] = gram_lo

    def forward(i):
        lanes = pl.ds(pl.multiple_of(i * pixels, pixels), pixels)
        wide = s.act[i]
        narrow = wide.astype(BF16)
        spread = nn(narrow, s.gram_hi[...]) + nn(narrow, s.gram_lo[...])
        var = jnp.sum(wide * spread, axis=-1, keepdims=True) / width
        token_rstd = lax.rsqrt(var + 1e-06)
        moved = nn(narrow, s.mixer[...]) * token_rstd
        value, slope = gelu_pair(moved + s.offsets[0:1, :])
        s.hid_t[:, lanes] = value.T.astype(BF16)
        s.act_t[:, lanes] = wide.T.astype(BF16)
        s.slope[i] = slope
        s.moved[i] = moved
        s.spread[i] = spread * (token_rstd / width)
        s.token_rstd[i] = jnp.broadcast_to(token_rstd, (pixels, 128))
        s.dhid[i] = jnp.zeros_like(slope)

    relay_near(3)
    beside(5)
    relay_far(2)
    every(n_chip, forward)
    s.patches_t[...] = s.patches[...].astype(F32).T.astype(BF16)

    def sib_copy(p):
        return send(s.sib_tx.at[p], s.sib_rx.at[p], s.sib_sem, p, p, sp=sibling)

    def down_out(q):
        swap, at = aim(q)
        p, slot = turn(q), swap * n_row + row_at
        return send(s.gd_tx.at[p], s.gd_rx.at[slot], s.gd_sem, p, slot, dp=row_first + at)

    def down_from(swap, act):
        def one(p):
            slot = swap * n_row + lax.rem(p, n_row)
            send(s.gd_tx.at[p], s.gd_rx.at[slot], s.gd_sem, p, slot, dp=p).wait_recv()
            act(s.gd_rx[slot].astype(F32))

        in_row(one)

    twin_out = send(s.gd_tx.at[twin], s.gd_twin, s.gd_sem, n_dp, n_dp, dp=twin)

    def block_of(q):
        p = turn(q)
        gate = s.mod[0:1, pl.ds(pl.multiple_of(2 * width + p * block, block), block)]
        cot = s.cot[p].reshape(n_chip * pixels, block)
        s.sib_tx[p] = (nn(s.hid_t[its_rows, :], cot) * gate).astype(BF16)
        sib_copy(p).start()
        s.gd_own[lax.rem(q, 2)] = nn(s.hid_t[my_rows, :], cot) * gate

        def part(h):
            rows = pl.ds(h * (n_chip // 2), n_chip // 2)
            tokens = s.cot[p, rows].reshape(n_chip // 2 * pixels, block)
            s.dhid[rows] += nt(tokens, s.gated[p]).reshape(n_chip // 2, pixels, 2 * hidden)

        every(2, part)

    def whole(q):
        p = turn(q)
        sib_copy(p).wait_recv()
        return p, s.gd_own[lax.rem(q, 2)] + s.sib_rx[p].astype(F32)

    def hand_over(q):
        p, total = whole(q)

        @pl.when(q < n_dp - 2)
        def _():
            s.gd_tx[p] = total.astype(BF16)
            down_out(q).start()

        @pl.when(q == n_dp - 2)
        def _():
            out_down[...] = total

            def add(value):
                out_down[...] += value

            down_from(1, add)
            s.gd_tx[twin] = out_down[...].astype(BF16)
            twin_out.start()

    @pl.loop(0, n_dp)
    def _(q):
        @pl.when(q + 6 < n_dp)
        def _():
            beside(q + 6)

        @pl.when(q + 4 < n_dp)
        def _():
            relay_near(q + 4)

        @pl.when(q + 3 < n_dp)
        def _():
            relay_far(q + 3)

        @pl.when(q > 0)
        def _():
            hand_over(q - 1)

        landed(q)
        block_of(q)

    s.du_sum[...] = jnp.zeros_like(s.du_sum)

    def backward(i):
        grad = s.dhid[i] * s.slope[i]
        s.du_sum[0:1, :] += jnp.sum(grad, axis=0, keepdims=True)
        grad = grad * s.token_rstd[i][:, 0:1]
        cross = jnp.sum(grad * s.moved[i], axis=-1, keepdims=True)
        narrow = grad.astype(BF16)
        s.du[pl.ds(pl.multiple_of(i * pixels, pixels), pixels), :] = narrow
        s.act[i] = nt(narrow, s.mixer[...]) - cross * s.spread[i]

    every(n_chip, backward)
    s.act[chip] += s.skip[...]

    def tile_of(p):
        rows = s.act[:, pl.ds(pl.multiple_of(p * 8, 8), 8), :]
        return rows.reshape(half, chans).astype(BF16)

    def part_copy(p, source):
        return send(s.part_tx.at[p], s.part_rx.at[source], s.part_sem, p, source, sp=p)

    def part_out(p):
        s.part_tx[p] = tile_of(p)
        part_copy(p, me).start()

    others(n_sp, me, part_out)
    s.part_rx[me] = tile_of(me)

    s.pairs[...] = nn(s.act_t[...], s.du[...])
    s.pair_tx[...] = s.pairs[:, its_cols].astype(BF16)
    s.sum_tx[...] = s.du_sum[:, its_cols]
    pair_copy = send(s.pair_tx, s.pair_rx, s.pair_sem, 3, 3, sp=sibling)
    pair_copy.start()
    sum_copy = send(s.sum_tx, s.sum_rx, s.pair_sem, 4, 4, sp=sibling)
    sum_copy.start()
    _, total = whole(n_dp - 1)
    out_down[...] = total

    pair_copy.wait_recv()
    sum_copy.wait_recv()
    s.q_tx[...] = (s.pairs[:, my_cols] + s.pair_rx[...].astype(F32)).astype(BF16)
    s.q_rx[image] = s.q_tx[...]
    du_sum = (s.du_sum[:, my_cols] + s.sum_rx[...])[0:1, :]

    def side_of(p):
        shift = s.mod[0:1, pl.ds(pl.multiple_of(p * block, block), block)]
        scale = s.mod[0:1, pl.ds(pl.multiple_of(width + p * block, block), block)]
        which = lax.broadcasted_iota(jnp.int32, (8, block), 0)
        return jnp.where(which == 2, du_sum, rows_of(1.0 + scale, shift, (8, block)))

    def q_copy(p, source):
        return send(s.q_tx, s.q_rx.at[source], s.q_sem, p, source, dp=p)

    def side_copy(p, source):
        return send(s.side_tx.at[p], s.side_rx.at[source], s.side_sem, p, source, dp=p)

    def forward_copy(p):
        at = lax.rem(p + n_row, n_dp)
        return send(s.q_rx.at[twin], s.q_rx.at[twin], s.q_sem, at, twin, dp=p)

    def side_out(p):
        s.side_tx[p] = side_of(p)
        side_copy(p, image).start()

    q_copy(twin, image).start()
    in_row(lambda p: q_copy(p, image).start())
    others(n_dp, image, side_out)
    s.side_rx[image] = side_of(image)

    others(n_sp, me, lambda p: part_copy(p, p).wait_recv())
    parts = []
    for k in range(2):
        total = s.part_rx[k].astype(F32)
        for j in range(1, n_chip):
            total = total + s.part_rx[2 * j + k].astype(F32)
        parts.append(total.reshape(n_chip, 1, pixels // n_sp, chans))
    dx = jnp.concatenate(parts, axis=1).reshape(pixels, chans) * s.slope0[...]
    s.slope0[...] = dx
    s.stat2_tx[...] = rows_of(
        jnp.sum(dx, axis=0, keepdims=True), jnp.sum(dx * s.z[...], axis=0, keepdims=True), (8, chans)
    )
    s.stat2_rx[me] = s.stat2_tx[...]

    def stat2_copy(p, source):
        return send(s.stat2_tx, s.stat2_rx.at[source], s.stat2_sem, p, source, sp=p)

    others(n_sp, me, lambda p: stat2_copy(p, me).start())

    q_copy(twin, twin).wait_recv()
    in_row(lambda p: forward_copy(p).start())

    others(n_sp, me, lambda p: stat2_copy(p, p).wait_recv())
    first, second = group_sums(s.stat2_rx)
    dz = (s.rstd[0:1, :] * (s.slope0[...] - first - s.z[...] * second)).astype(BF16)
    s.grad[...] = nn(s.patches_t[...], dz)

    def rows_at(k):
        return pl.ds(pl.multiple_of(k * taps, 8), taps)

    n_half = 2
    lanes_of = lambda h: slice(h * (chans // n_half), (h + 1) * (chans // n_half))

    def grad_copy(h, p, source):
        at = h * n_sp
        return send(s.grad_tx.at[h, p], s.grad_rx.at[h, source], s.grad_sem, at + p, at + source, sp=p)

    def all_copy(h, p, source):
        at = h * n_dp
        return send(s.all_tx.at[h], s.all_rx.at[h, source], s.all_sem, at + p, at + source, dp=p)

    def last_copy(h, p, source):
        at = h * n_sp
        return send(s.last_tx.at[h], s.last_rx.at[h, source], s.last_sem, at + p, at + source, sp=p)

    for h in range(n_half):

        def grad_out(p, h=h):
            s.grad_tx[h, p] = s.grad[rows_at(p), lanes_of(h)].astype(BF16)
            grad_copy(h, p, me).start()

        others(n_sp, me, grad_out)
        s.grad_rx[h, me] = s.grad[rows_at(me), lanes_of(h)].astype(BF16)

    def slots(ref, h, n):
        total = ref[h, 0].astype(F32)
        for j in range(1, n):
            total = total + ref[h, j].astype(F32)
        return total

    for h in range(n_half):
        others(n_sp, me, lambda p: grad_copy(h, p, p).wait_recv())
        s.all_tx[h] = slots(s.grad_rx, h, n_sp).astype(BF16)
        s.all_rx[h, image] = s.all_tx[h]
        others(n_dp, image, lambda p: all_copy(h, p, image).start())

    for h in range(n_half):
        others(n_dp, image, lambda p: all_copy(h, p, p).wait_recv())
        s.last_tx[h] = slots(s.all_rx, h, n_dp).astype(BF16)
        s.last_rx[h, me] = s.last_tx[h]
        others(n_sp, me, lambda p: last_copy(h, p, me).start())

    def add_down(value):
        out_down[...] += value

    down_from(0, add_down)
    twin_out.wait_recv()
    add_down(s.gd_twin[...].astype(F32))

    in_row(lambda p: q_copy(p, p).wait_recv())
    in_row(lambda p: q_copy(p, lax.rem(p + n_row, n_dp)).wait_recv())
    others(n_dp, image, lambda p: side_copy(p, p).wait_recv())
    here = s.emb[:, pl.ds(pl.multiple_of(image * block, block), block)].astype(F32) - mean_col
    here_t = here.T
    s.emb_t[...] = here_t
    which = lax.broadcasted_iota(jnp.int32, (n_dp, block), 0)
    shifts = jnp.zeros((n_dp, block), F32)
    sums = jnp.zeros((n_dp, block), F32)
    for k in range(n_dp):
        shifts = jnp.where(which == k, s.side_rx[k, 1:2, :], shifts)
        sums = jnp.where(which == k, s.side_rx[k, 2:3, :], sums)
    out_up[...] = exact(shifts, sums, ((0,), (0,)))

    def up_part(k):
        left = here_t * s.side_rx[k].T[:, 0:1]
        out_up[...] += nn(left.astype(BF16), s.q_rx[k])

    for k in range(n_dp):
        up_part(k)

    for h in range(n_half):
        others(n_sp, me, lambda p: last_copy(h, p, p).wait_recv())

        def show(k, h=h):
            out_conv[rows_at(k), lanes_of(h)] = s.last_rx[h, k].astype(F32)

        every(n_sp, show)

    for copy in (mix_copy, off_copy, pair_copy, sum_copy):
        copy.wait_send()

    @pl.when(me < n_sp - 1)
    def _():
        rim_copy.wait_send()

    def left(p):
        for copy in (stat_copy(p), act_copy(p, me), part_copy(p, me), stat2_copy(p, me)):
            copy.wait_send()
        for h in range(n_half):
            grad_copy(h, p, me).wait_send()
            last_copy(h, p, me).wait_send()

    others(n_sp, me, left)

    def left_dp(p):
        for copy in (q_copy(p, image), side_copy(p, image)):
            copy.wait_send()
        for h in range(n_half):
            all_copy(h, p, image).wait_send()

    others(n_dp, image, left_dp)

    every(n_dp - 2, lambda q: down_out(q).wait_send())
    twin_out.wait_send()

    def left_block(p):
        sib_copy(p).wait_send()
        for name in routes:
            cot_copy(name, p).wait_send()

    every(n_dp, left_block)


class Scratch:
    def __init__(self, names, refs):
        for name, ref in zip(names, refs):
            setattr(self, name, ref)


def on_device(
    n_sp, n_dp, feats, conv_w, group_norm_gain, group_norm_bias, emb_w, time_w, up_w, down_w, steps, cotangent
):
    image = feats[0]
    rows_in, cols_in, in_chans = image.shape
    rows, cols = rows_in // 2, cols_in // 2
    pixels = rows * cols
    planes = image.reshape(rows, 2, cols, 2, in_chans).transpose(1, 3, 0, 2, 4)
    freq_count = time_w.shape[0] // 2
    freqs = jnp.exp(-math.log(10000.0) * jnp.arange(freq_count, dtype=F32) / freq_count)
    angle = steps[0].astype(F32) * freqs
    embed = jax.nn.silu(jnp.concatenate([jnp.cos(angle), jnp.sin(angle)])).astype(BF16)
    es = jnp.broadcast_to(embed[None, :], (16, embed.shape[0]))
    chans = conv_w.shape[1]
    width = emb_w.shape[1]
    hidden = up_w.shape[1]
    block = width // n_dp
    n_chip = n_sp // 2
    taps = conv_w.shape[0] // n_sp
    half = pixels // 2
    tokens = n_chip * pixels
    vm = pltpu.VMEM
    dma = lambda n: pltpu.SemaphoreType.DMA((2, n))
    scratch = dict(
        load=pltpu.SemaphoreType.DMA((8 + 2 * n_dp + time_w.shape[1] // 1024,)),
        stat_sem=dma(n_sp), act_sem=dma(n_sp), part_sem=dma(n_sp), stat2_sem=dma(n_sp),
        grad_sem=dma(2 * n_sp), last_sem=dma(2 * n_sp), cot_sem=dma(12 * n_dp), pair_sem=dma(8),
        sib_sem=dma(n_dp), gd_sem=dma(n_dp + 1), q_sem=dma(n_dp), side_sem=dma(n_dp), all_sem=dma(2 * n_dp),
        patches=vm((pixels, 9 * in_chans), BF16), rim_tx=vm((2, rows, in_chans), BF16),
        rim_rx=vm((2, rows, in_chans), BF16), conv=vm(conv_w.shape, BF16), emb=vm(emb_w.shape, BF16),
        time=vm((time_w.shape[1] // 1024, time_w.shape[0], 1024), BF16), up=vm(up_w.shape, BF16),
        gated=vm((n_dp, 2 * hidden, block), BF16), cot=vm((n_dp, n_chip, pixels, block), BF16),
        z=vm((pixels, chans), F32), slope0=vm((pixels, chans), F32), rstd=vm((8, chans), F32),
        stat_tx=vm((8, chans), F32), stat_rx=vm((n_sp, 8, chans), F32),
        stat2_tx=vm((8, chans), F32), stat2_rx=vm((n_sp, 8, chans), F32),
        mod=vm((16, 3 * width), F32), act_tx=vm((2, half, chans), BF16),
        act_rx=vm((n_sp, half, chans), BF16), act=vm((n_chip, pixels, chans), F32),
        act_t=vm((chans, tokens), BF16), mean_col=vm((chans, 128), F32), gram=vm((chans, chans), F32),
        gram_hi=vm((chans, chans), BF16), gram_lo=vm((chans, chans), BF16),
        mix=vm((chans, hidden), F32), mixer=vm((chans, 2 * hidden), BF16),
        offset=vm((16, hidden), F32), offsets=vm((16, 2 * hidden), F32), skip=vm((pixels, chans), F32),
        hid_t=vm((2 * hidden, tokens), BF16), slope=vm((n_chip, pixels, 2 * hidden), F32),
        moved=vm((n_chip, pixels, 2 * hidden), F32), dhid=vm((n_chip, pixels, 2 * hidden), F32),
        spread=vm((n_chip, pixels, chans), F32), token_rstd=vm((n_chip, pixels, 128), F32),
        patches_t=vm((9 * in_chans, pixels), BF16),
        sib_tx=vm((n_dp, hidden, block), BF16), sib_rx=vm((n_dp, hidden, block), BF16),
        gd_own=vm((2, hidden, block), F32), gd_tx=vm((n_dp, hidden, block), BF16),
        gd_rx=vm((n_dp, hidden, block), BF16), gd_twin=vm((hidden, block), BF16), du_sum=vm((8, 2 * hidden), F32),
        du=vm((tokens, 2 * hidden), BF16), part_tx=vm((n_sp, half, chans), BF16),
        part_rx=vm((n_sp, half, chans), BF16), pairs=vm((chans, 2 * hidden), F32),
        pair_tx=vm((chans, hidden), BF16), pair_rx=vm((chans, hidden), BF16),
        sum_tx=vm((8, hidden), F32), sum_rx=vm((8, hidden), F32), q_tx=vm((chans, hidden), BF16),
        q_rx=vm((n_dp, chans, hidden), BF16), side_tx=vm((n_dp, 8, block), F32),
        side_rx=vm((n_dp, 8, block), F32), grad=vm((conv_w.shape[0], chans), F32),
        grad_tx=vm((2, n_sp, taps, chans // 2), BF16), grad_rx=vm((2, n_sp, taps, chans // 2), BF16),
        all_tx=vm((2, taps, chans // 2), BF16), all_rx=vm((2, n_dp, taps, chans // 2), BF16),
        last_tx=vm((2, taps, chans // 2), BF16), last_rx=vm((2, n_sp, taps, chans // 2), BF16),
        emb_t=vm((block, chans), F32),
    )
    names = tuple(scratch)

    def kernel(*refs):
        body(n_sp, n_dp, *refs[:13], Scratch(names, refs[13:]))

    in_vmem = pl.BlockSpec(memory_space=pltpu.VMEM)
    in_place = pl.BlockSpec(memory_space=pl.ANY)
    return pl.pallas_call(
        kernel,
        out_shape=(
            jax.ShapeDtypeStruct(conv_w.shape, F32),
            jax.ShapeDtypeStruct((block, hidden), F32),
            jax.ShapeDtypeStruct((hidden, block), F32),
        ),
        in_specs=[in_vmem] * 4 + [in_place] * 6,
        out_specs=(in_vmem,) * 3,
        scratch_shapes=list(scratch.values()),
        compiler_params=pltpu.CompilerParams(
            collective_id=0, has_side_effects=True, vmem_limit_bytes=67043328
        ),
    )(es, group_norm_gain[None], group_norm_bias[None], planes, conv_w, emb_w, time_w, up_w, down_w, cotangent[0])


def solution(mesh):
    in_specs = (
        P("dp", None, "sp", None),
        P(),
        P(),
        P(),
        P(),
        P(),
        P(None, "sp"),
        P("sp", None),
        P("dp"),
        P("dp", "sp", None),
    )
    out_specs = (P(), P("dp", "sp"), P("sp", "dp"))
    return jax.shard_map(
        functools.partial(on_device, mesh.shape["sp"], mesh.shape["dp"]),
        mesh=mesh,
        in_specs=in_specs,
        out_specs=out_specs,
        check_vma=False,
    )
```
